256 devices in a mesh: line: 8 (over z_hi, core), dp: 32 (over z_lo, x, y).
Axes of the slice: x: 4, y: 4, z: 8 (z_hi: 4, z_lo: 2; z = z_hi * 2 + z_lo), core: 2. Of those that a mesh axis runs over, the one named last changes fastest.
Arguments:
- fields: bfloat16 [32, 4096, 128], P('dp', 'line'), may hold values from -6 to 6
- cotangent: bfloat16 [32, 4096, 128], P('dp', 'line'), may hold values from -6 to 6
- norm_gain: float32 [3, 128], replicated, may hold values from 0.1 to 1.9
- kernel: float32 [3, 15, 128], replicated, may hold values from -1.8 to 1.8
- mix_weight: bfloat16 [3, 128, 128], replicated, may hold values from -0.5 to 0.5
- line_order: int32 [3, 4096], P(None, 'line'), may hold values from 0 to 511, as said below
- line_starts: int32 [3, 32], P(None, 'line'), may hold values from 0 to 32
Outputs:
- imitated: bfloat16 [32, 4096, 128], P('dp', 'line')
- field_grad: bfloat16 [32, 4096, 128], P('dp', 'line')
- mix_grad: float32 [3, 128, 128], replicated
- kernel_grad: float32 [3, 15, 128], replicated
- gain_grad: float32 [3, 128], replicated
The draws below stay inside these ranges and needn't reach their ends.
Inputs may be any that keep to these rules, and one draw needn't show every extreme that they name: For each direction, every aligned block of 512 entries of line_order is a permutation of 0 to 511.
All inputs are finite; a program needn't handle non-finite values.
Results may differ from the reference program's by a relative error of at most 0.014.
Values may be sent and summed in bfloat16 or wider, within the bound.
No kernel may reach another device: no remote copies, remote signals or barrier semaphores. Data moves between devices by JAX's collectives and lax.ppermute only.
A program may use at most 64 MiB of HBM per device.

```python
import jax
import jax.numpy as jnp
from jax import lax

C = 128
LINE = 128
TAPS = 15
CELL_DEV = 512
SAMPLES = 32
NCELL = 4096
NLINES = 32
N_LINE = 8


def draw_line_order(key, part):
    holders = NCELL // CELL_DEV
    keys = jax.random.split(jax.random.fold_in(key, 17), 3 * holders)
    tables = jax.vmap(lambda single_key: jax.random.permutation(single_key, CELL_DEV))(keys)
    return tables.reshape(3, NCELL).astype(jnp.int32)


def with_ends(result, stream_key, smallest, largest):
    extent = result.shape
    index_at = [jax.random.randint(jax.random.fold_in(stream_key, axis), (), 0, extent[axis]) for axis in range(len(extent))]
    result = result.at[tuple(index_at)].set(smallest)
    longest = extent.index(max(extent))
    index_at[longest] = (index_at[longest] + 1) % extent[longest]
    return result.at[tuple(index_at)].set(largest)


def block_levels(key, shape, pieces, least, top_value):
    gain = 1.0
    for dim, shards_of in pieces:
        draws = jax.random.uniform(jax.random.fold_in(jax.random.fold_in(key, 6), dim), (shards_of,), jnp.float32, least / len(pieces), top_value / len(pieces))
        gain = gain * jnp.repeat(jnp.exp(draws), shape[dim] // shards_of).reshape((-1,) + (1,) * (len(shape) - 1 - dim))
    return gain


def normal_values(stream_key, shape, deviation, bound, cuts=(), held_as=jnp.bfloat16):
    loudness = block_levels(stream_key, shape, cuts, -0.22, 0.18) if cuts else 1.0
    array = jax.random.normal(stream_key, shape, jnp.float32) * deviation * loudness
    return jnp.minimum(jnp.maximum(array, -bound), bound).astype(held_as)


def setup_inputs(seed: int = 0) -> dict:
    splits = jax.random.split(jax.random.key(seed), 8)
    fields = normal_values(splits[0], (SAMPLES, NCELL, C), 1.0, 6.0, ((0, 32), (1, 8)))
    cotangent = normal_values(splits[1], (SAMPLES, NCELL, C), 1.0, 6.0, ((0, 32), (1, 8)))
    norm_gain = jnp.clip(1.0 + 0.18 * jax.random.normal(splits[2], (3, C), jnp.float32), 0.1, 1.9)
    kernel = normal_values(splits[3], (3, TAPS, C), 0.3, 1.8, (), jnp.float32)
    mix_weight = normal_values(splits[4], (3, C, C), C ** -0.5, 0.5)
    line_order = draw_line_order(jax.random.fold_in(splits[7], 71), 0)
    line_starts = with_ends(jax.random.randint(splits[6], (3, NLINES), 0, 33), jax.random.fold_in(splits[6], 1), 0, 32).astype(jnp.int32)
    return {"fields": fields, "cotangent": cotangent, "norm_gain": norm_gain, "kernel": kernel, "mix_weight": mix_weight, "line_order": line_order, "line_starts": line_starts}


EPSILON = 1e-06

def tap_offsets():
    offsets = [0]
    for dilation_level in range(7):
        offsets = offsets + [-2 ** dilation_level, 2 ** dilation_level]
    return offsets

def shifted(values, offset):
    if offset > 0:
        return jnp.concatenate([values[:, offset:], jnp.zeros_like(values[:, :offset])], axis=1)
    if offset < 0:
        return jnp.concatenate([jnp.zeros_like(values[:, offset:]), values[:, :offset]], axis=1)
    return values

def depthwise(inputs, weights):
    running = jnp.zeros(inputs.shape, jnp.float32)
    for tap_index, offset in enumerate(tap_offsets()):
        running = running + weights[tap_index] * shifted(inputs, offset)
    return running

def depthwise_transpose(grads, weights):
    running = jnp.zeros(grads.shape, jnp.float32)
    for tap_index, offset in enumerate(tap_offsets()):
        running = running + weights[tap_index] * shifted(grads, -offset)
    return running

def kernel_terms(grads, inputs):
    return jnp.stack([lax.optimization_barrier(jnp.sum(grads * shifted(inputs, offset), axis=(0, 1))) for offset in tap_offsets()])

def sources(line_order, direction):
    piece_len = CELL_DEV // N_LINE
    position = jnp.arange(NCELL, dtype=jnp.int32)
    holder = position // CELL_DEV
    entries = line_order[direction]
    anchor = entries // piece_len
    within = entries % piece_len
    blocks_at = (holder - direction * anchor) % N_LINE
    return (anchor * CELL_DEV + blocks_at * piece_len + within).astype(jnp.int32)

def keep_lines(line_starts, direction):
    position = jnp.arange(LINE, dtype=jnp.int32)
    return position[None, :] >= line_starts[direction][:, None]

def one_sample(sample, grad_out, norm_gain, kernel, mix_weight, gathers, scatters, masks):
    stream = sample
    saved = []
    for direction in range(3):
        values = stream.astype(jnp.float32)
        inverse = lax.rsqrt(lax.optimization_barrier(jnp.mean(values * values, axis=-1, keepdims=True)) + EPSILON)
        scaled = values * inverse
        normed = (scaled * norm_gain[direction]).astype(jnp.bfloat16)
        regrouped = normed[gathers[direction]].reshape(NLINES, LINE, C)
        masked = jnp.where(masks[direction][:, :, None], regrouped, jnp.zeros_like(regrouped))
        hidden = depthwise(masked.astype(jnp.float32), kernel[direction])
        activated = jax.nn.silu(hidden).astype(jnp.bfloat16)
        mixed = jnp.dot(activated.reshape(NCELL, C), mix_weight[direction], preferred_element_type=jnp.float32).astype(jnp.bfloat16)
        stream = (values + mixed[scatters[direction]].astype(jnp.float32)).astype(jnp.bfloat16)
        saved.append((inverse, scaled, masked, hidden, activated))
    grad_stream = grad_out
    mix_list = [None, None, None]
    kernel_list = [None, None, None]
    gain_list = [None, None, None]
    for direction in (2, 1, 0):
        inverse, scaled, masked, hidden, activated = saved[direction]
        grad_mixed = grad_stream[gathers[direction]]
        mix_list[direction] = jnp.dot(activated.reshape(NCELL, C).T, grad_mixed, preferred_element_type=jnp.float32)
        grad_act = jnp.dot(grad_mixed, mix_weight[direction].T, preferred_element_type=jnp.float32).reshape(NLINES, LINE, C)
        gate_value = jax.nn.sigmoid(hidden)
        grad_hidden = (grad_act * (gate_value * (1.0 + hidden * (1.0 - gate_value)))).astype(jnp.bfloat16)
        hidden_grad_f = grad_hidden.astype(jnp.float32)
        kernel_list[direction] = kernel_terms(hidden_grad_f, masked.astype(jnp.float32))
        grad_masked = depthwise_transpose(hidden_grad_f, kernel[direction])
        grad_normed = jnp.where(masks[direction][:, :, None], grad_masked, jnp.zeros_like(grad_masked)).astype(jnp.bfloat16)
        grad_cells = grad_normed.reshape(NCELL, C)[scatters[direction]].astype(jnp.float32)
        gain_list[direction] = lax.optimization_barrier(jnp.sum(grad_cells * scaled, axis=0))
        weighted = grad_cells * norm_gain[direction]
        grad_norm = inverse * (weighted - scaled * lax.optimization_barrier(jnp.mean(weighted * scaled, axis=-1, keepdims=True)))
        grad_stream = (grad_stream.astype(jnp.float32) + grad_norm).astype(jnp.bfloat16)
    return (stream, grad_stream, jnp.stack(mix_list), jnp.stack(kernel_list), jnp.stack(gain_list))

def reference(fields, cotangent, norm_gain, kernel, mix_weight, line_order, line_starts):
    gathers = [sources(line_order, direction) for direction in range(3)]
    scatters = [jnp.zeros((NCELL,), jnp.int32).at[gathers[direction]].set(jnp.arange(NCELL, dtype=jnp.int32)) for direction in range(3)]
    masks = [keep_lines(line_starts, direction) for direction in range(3)]

    def run_sample(sample_pair):
        return one_sample(sample_pair[0], sample_pair[1], norm_gain, kernel, mix_weight, gathers, scatters, masks)
    imitated, field_grad, mix_parts, kernel_parts, gain_parts = lax.map(run_sample, (fields, cotangent))
    grad_scale = float(SAMPLES * NCELL) ** (-0.5)
    mix_grad = lax.optimization_barrier(jnp.sum(mix_parts, axis=0)) * grad_scale
    kernel_grad = lax.optimization_barrier(jnp.sum(kernel_parts, axis=0)) * grad_scale
    gain_grad = lax.optimization_barrier(jnp.sum(gain_parts, axis=0)) * grad_scale
    return (imitated, field_grad, mix_grad, kernel_grad, gain_grad)
```

```python
import functools

import jax
import jax.numpy as jnp
from jax import lax
from jax.experimental import pallas as pl
from jax.experimental.pallas import tpu as pltpu
from jax.sharding import PartitionSpec as P

LINE = 128
CH = 128
TAPS = 15
CELLS = 512
NL = 8
Q = CELLS // NL
LINES = CELLS // LINE
EPSILON = 1e-06
OFFSETS = [0] + [s * 2**level for level in range(7) for s in (-1, 1)]
F32 = jnp.float32
BF16 = jnp.bfloat16
ROWS = LINE + TAPS + 1


def dot(a, b, ca, cb):
    return lax.dot_general(a, b, (((ca,), (cb,)), ((), ())), preferred_element_type=F32)


def slot_row(order_row, sign):
    if sign == 0:
        return order_row
    me = lax.axis_index("line")
    home = lax.shift_right_logical(order_row, 6)
    within = jnp.bitwise_and(order_row, Q - 1)
    slot = jnp.bitwise_and(me + sign * home + NL, NL - 1)
    return slot * Q + within


def picks(row, line):
    part = row[:, line * LINE : (line + 1) * LINE]
    wanted = jnp.transpose(jnp.broadcast_to(part, (LINE, LINE)))
    lanes = lax.broadcasted_iota(jnp.int32, (LINE, LINE), 1)
    return jnp.concatenate(
        [jnp.where(wanted == lanes + c * LINE, 1.0, 0.0).astype(BF16) for c in range(LINES)],
        axis=1,
    )


def place(row, values):
    wanted = jnp.broadcast_to(row, (LINE, CELLS))
    out = []
    for c in range(LINES):
        rows = lax.broadcasted_iota(jnp.int32, (LINE, CELLS), 0) + c * LINE
        hot = jnp.where(wanted == rows, 1.0, 0.0).astype(BF16)
        out.append(dot(hot, values, 1, 0).astype(BF16))
    return out


def put(ref, first, blocks):
    for c, block in enumerate(blocks):
        for h in range(LINE // Q):
            ref[c * (LINE // Q) + h, first : first + Q, :] = block[h * Q : (h + 1) * Q]


def shifts(pad, values):
    pad[8 : 8 + LINE, :] = values
    for offset in OFFSETS:
        if offset == 0:
            yield values
        elif abs(offset) < 8:
            yield pad[8 + offset : 8 + offset + LINE, :]
        elif offset > 0:
            yield jnp.concatenate([values[offset:], jnp.zeros((offset, CH), F32)], axis=0)
        else:
            yield jnp.concatenate([jnp.zeros((-offset, CH), F32), values[:offset]], axis=0)


def clear(pad):
    pad[0:8, :] = jnp.zeros((8, CH), F32)
    pad[8 + LINE : 16 + LINE, :] = jnp.zeros((8, CH), F32)


def norm(x, gain, start):
    inverse = lax.rsqrt(jnp.mean(x * x, axis=-1, keepdims=True) + EPSILON)
    scaled = x * inverse
    normed = (scaled * gain).astype(BF16).astype(F32)
    keep = lax.broadcasted_iota(jnp.int32, (LINE, CH), 0) >= start
    return inverse, scaled, jnp.where(keep, normed, 0.0), keep


def conv(pad, masked, taps):
    total = None
    for t, moved in enumerate(shifts(pad, masked)):
        term = taps[t : t + 1, :] * moved
        total = term if total is None else total + term
    return total


def sigmoid(h):
    return 1.0 / (1.0 + jnp.exp(-h))


def forward_line(k, line, x, starts, gain_ref, taps_ref, mix_ref, pad):
    inverse, scaled, masked, keep = norm(x, gain_ref[k : k + 1, :], starts[k, line])
    hidden = conv(pad, masked, taps_ref[k])
    gate = sigmoid(hidden)
    active = (hidden * gate).astype(BF16)
    mixed = dot(active, mix_ref[k], 1, 0).astype(BF16).astype(F32)
    after = (x + mixed).astype(BF16)
    return inverse, scaled, masked, keep, hidden, gate, active, after


def backward_line(k, grad, state, gain_ref, taps_ref, mix_ref, pad, sums):
    inverse, scaled, masked, keep, hidden, gate, active = state
    gain = gain_ref[k : k + 1, :]
    taps = taps_ref[k]
    sums["mix"] = sums["mix"] + dot(active, grad, 0, 0)
    grad_act = dot(grad, mix_ref[k], 1, 1)
    grad_hidden = (grad_act * (gate * (1.0 + hidden * (1.0 - gate)))).astype(BF16).astype(F32)
    total = None
    for t, moved in enumerate(shifts(pad, grad_hidden)):
        u = t if t == 0 else (t + 1 if t % 2 else t - 1)
        term = taps[u : u + 1, :] * moved
        total = term if total is None else total + term
        part = jnp.sum((moved * masked).reshape(LINE // 8, 8, CH), axis=0)
        sums["taps"][u] = part if sums["taps"][u] is None else sums["taps"][u] + part
    cells = jnp.where(keep, total, 0.0).astype(BF16).astype(F32)
    part = jnp.sum((cells * scaled).reshape(LINE // 8, 8, CH), axis=0)
    sums["gain"] = part if sums["gain"] is None else sums["gain"] + part
    weighted = cells * gain
    moved = inverse * (weighted - scaled * jnp.mean(weighted * scaled, axis=-1, keepdims=True))
    return (grad.astype(F32) + moved).astype(BF16)


def new_sums():
    return {"mix": jnp.zeros((CH, CH), F32), "taps": [None] * TAPS, "gain": None}


def write_sums(ref, sums):
    ref[0:CH, :] = sums["mix"]
    rows = [jnp.sum(part, axis=0, keepdims=True) for part in sums["taps"]]
    rows.append(jnp.sum(sums["gain"], axis=0, keepdims=True))
    ref[CH:ROWS, :] = jnp.concatenate(rows, axis=0)


def prep_kernel(fields_ref, cot_ref, out_ref):
    me = lax.axis_index("line")
    for b in range(NL):
        out_ref[b, 0:Q, :] = fields_ref[0, b * Q : (b + 1) * Q, :]
        slot = jnp.bitwise_and(b + 2 * me, NL - 1)
        out_ref[pl.ds(slot, 1), Q : 2 * Q, :] = cot_ref[:, b * Q : (b + 1) * Q, :]


def forward_kernel(k, starts, in_ref, gain_ref, taps_ref, mix_ref, order_ref, out_ref, x_ref, h_ref, pad):
    clear(pad)
    received = in_ref[:, 0:Q, :].reshape(CELLS, CH)
    order = order_ref[k : k + 1, :]
    row = slot_row(order, 0 if k == 0 else -1)
    after = []
    for line in range(LINES):
        x = dot(picks(row, line), received, 1, 0)
        done = forward_line(k, line, x, starts, gain_ref, taps_ref, mix_ref, pad)
        x_ref[line] = x.astype(BF16)
        h_ref[line] = done[4]
        after.append(done[7])
    put(out_ref, 0, place(slot_row(order, 1), jnp.concatenate(after, axis=0)))


def turn_kernel(starts, in_ref, cot_ref, gain_ref, taps_ref, mix_ref, order_ref, out_ref, sum_ref, pad):
    k = 2
    clear(pad)
    received = in_ref[...].reshape(CELLS, CH)
    cot = cot_ref[:, Q : 2 * Q, :].reshape(CELLS, CH)
    order = order_ref[k : k + 1, :]
    row = slot_row(order, -1)
    sums = new_sums()
    after, grads = [], []
    for line in range(LINES):
        x = dot(picks(row, line), received, 1, 0)
        done = forward_line(k, line, x, starts, gain_ref, taps_ref, mix_ref, pad)
        after.append(done[7])
        grad = dot(picks(order, line), cot, 1, 0).astype(BF16)
        grads.append(backward_line(k, grad, done[:7], gain_ref, taps_ref, mix_ref, pad, sums))
    put(out_ref, 0, place(order, jnp.concatenate(after, axis=0)))
    put(out_ref, Q, place(row, jnp.concatenate(grads, axis=0)))
    write_sums(sum_ref, sums)


def backward_kernel(k, starts, in_ref, x_ref, h_ref, gain_ref, taps_ref, mix_ref, order_ref, out_ref, sum_ref, *rest):
    pad = rest[-1]
    clear(pad)
    if k == 1:
        me = lax.axis_index("line")
        for b in range(NL):
            slot = jnp.bitwise_and(b + 2 * me, NL - 1)
            rest[0][:, b * Q : (b + 1) * Q, :] = in_ref[pl.ds(slot, 1), 0:Q, :]
        received = in_ref[:, Q : 2 * Q, :].reshape(CELLS, CH)
    else:
        received = in_ref[...].reshape(CELLS, CH)
    order = order_ref[k : k + 1, :]
    row = slot_row(order, 1)
    sums = new_sums()
    grads = []
    for line in range(LINES):
        grad = dot(picks(row, line), received, 1, 0).astype(BF16)
        x = x_ref[line].astype(F32)
        hidden = h_ref[line]
        inverse, scaled, masked, keep = norm(x, gain_ref[k : k + 1, :], starts[k, line])
        gate = sigmoid(hidden)
        active = (hidden * gate).astype(BF16)
        state = (inverse, scaled, masked, keep, hidden, gate, active)
        grads.append(backward_line(k, grad, state, gain_ref, taps_ref, mix_ref, pad, sums))
    put(out_ref, 0, place(slot_row(order, -1 if k else 0), jnp.concatenate(grads, axis=0)))
    write_sums(sum_ref, sums)


def call(kernel, outs, name, n_in):
    smem = pl.BlockSpec(memory_space=pltpu.SMEM)
    vmem = pl.BlockSpec(memory_space=pltpu.VMEM)
    return pl.pallas_call(
        kernel,
        out_shape=outs,
        in_specs=([smem] if n_in > 2 else [vmem]) + [vmem] * (n_in - 1),
        out_specs=[vmem] * len(outs),
        scratch_shapes=[pltpu.VMEM((LINE + 16, CH), F32)] if n_in > 2 else [],
        name=name,
    )


def shape(*dims, dtype=BF16):
    return jax.ShapeDtypeStruct(dims, dtype)


def exchange(blocks):
    return lax.all_to_all(blocks, "line", split_axis=0, concat_axis=0, tiled=True)


def body(fields, cotangent, norm_gain, kernel, mix_weight, line_order, line_starts):
    dp_size = lax.axis_size("dp")
    weights = (norm_gain, kernel, mix_weight, line_order)
    state = (shape(LINES, LINE, CH), shape(LINES, LINE, CH, dtype=F32))
    sums = shape(ROWS, CH, dtype=F32)
    blocks = shape(NL, Q, CH)
    (packed,) = call(prep_kernel, (shape(NL, 2 * Q, CH),), "prep", 2)(fields, cotangent)
    first = exchange(packed)
    moved, x0, h0 = call(functools.partial(forward_kernel, 0), (blocks, *state), "fwd0", 6)(
        line_starts, first, *weights
    )
    moved, x1, h1 = call(functools.partial(forward_kernel, 1), (blocks, *state), "fwd1", 6)(
        line_starts, exchange(moved), *weights
    )
    moved, sums2 = call(turn_kernel, (shape(NL, 2 * Q, CH), sums), "turn", 7)(
        line_starts, exchange(moved), first, *weights
    )
    moved, sums1, imitated = call(
        functools.partial(backward_kernel, 1), (blocks, sums, shape(1, CELLS, CH)), "bwd1", 8
    )(line_starts, exchange(moved), x1, h1, *weights)
    moved, sums0 = call(functools.partial(backward_kernel, 0), (blocks, sums), "bwd0", 8)(
        line_starts, exchange(moved), x0, h0, *weights
    )
    field_grad = exchange(moved).reshape(1, CELLS, CH)
    grad_scale = float(dp_size * NL * CELLS) ** (-0.5)
    total = jnp.stack([sums0, sums1, sums2]).reshape(NL, 3 * ROWS // NL, CH)
    part = jnp.sum(exchange(total), axis=0)
    step = 1
    while step < dp_size:
        pairs = [(i, i ^ step) for i in range(dp_size)]
        part = part + lax.ppermute(part, "dp", pairs)
        step *= 2
    whole = jnp.broadcast_to((part * grad_scale)[None], (NL, 3 * ROWS // NL, CH))
    whole = exchange(whole).reshape(3, ROWS, CH)
    return (
        imitated,
        field_grad,
        whole[:, :CH],
        whole[:, CH : CH + TAPS],
        whole[:, CH + TAPS],
    )


def solution(mesh):
    in_specs = (
        P("dp", "line", None),
        P("dp", "line", None),
        P(),
        P(),
        P(),
        P(None, "line"),
        P(None, "line"),
    )
    out_specs = (P("dp", "line", None), P("dp", "line", None), P(), P(), P())
    return jax.shard_map(body, mesh=mesh, in_specs=in_specs, out_specs=out_specs, check_vma=False)
```

```python
import functools

import jax
import jax.numpy as jnp
from jax import lax
from jax.experimental import pallas as pl
from jax.experimental.pallas import tpu as pltpu
from jax.sharding import PartitionSpec as P

LINE = 128
CH = 128
TAPS = 15
CELLS = 512
NL = 8
Q = CELLS // NL
LINES = CELLS // LINE
EPSILON = 1e-06
OFFSETS = [0] + [s * 2**level for level in range(7) for s in (-1, 1)]
F32 = jnp.float32
BF16 = jnp.bfloat16
ROWS = LINE + TAPS + 1
VMEM_GRANT = 8 * 2**20
CHIPS = NL // 2
SHARE = 56


def dot(a, b, ca, cb):
    return lax.dot_general(a, b, (((ca,), (cb,)), ((), ())), preferred_element_type=F32)


def slot_row(order_row, sign):
    if sign == 0:
        return order_row
    me = lax.axis_index("line")
    home = lax.shift_right_logical(order_row, 6)
    within = jnp.bitwise_and(order_row, Q - 1)
    slot = jnp.bitwise_and(me + sign * home + NL, NL - 1)
    return slot * Q + within


def picks(row, line):
    part = row[:, line * LINE : (line + 1) * LINE]
    wanted = jnp.transpose(jnp.broadcast_to(part, (LINE, LINE)))
    lanes = lax.broadcasted_iota(jnp.int32, (LINE, LINE), 1)
    return jnp.concatenate(
        [jnp.where(wanted == lanes + c * LINE, 1.0, 0.0).astype(BF16) for c in range(LINES)],
        axis=1,
    )


def place(row, values):
    wanted = jnp.broadcast_to(row, (LINE, CELLS))
    out = []
    for c in range(LINES):
        rows = lax.broadcasted_iota(jnp.int32, (LINE, CELLS), 0) + c * LINE
        hot = jnp.where(wanted == rows, 1.0, 0.0).astype(BF16)
        out.append(dot(hot, values, 1, 0).astype(BF16))
    return out


def put(ref, first, blocks):
    for c, block in enumerate(blocks):
        for h in range(LINE // Q):
            ref[c * (LINE // Q) + h, first : first + Q, :] = block[h * Q : (h + 1) * Q]


def shifts(pad, values):
    pad[8 : 8 + LINE, :] = values
    for offset in OFFSETS:
        if offset == 0:
            yield values
        elif abs(offset) < 8:
            yield pad[8 + offset : 8 + offset + LINE, :]
        elif offset > 0:
            yield jnp.concatenate([values[offset:], jnp.zeros((offset, CH), F32)], axis=0)
        else:
            yield jnp.concatenate([jnp.zeros((-offset, CH), F32), values[:offset]], axis=0)


def clear(pad):
    pad[0:8, :] = jnp.zeros((8, CH), F32)
    pad[8 + LINE : 16 + LINE, :] = jnp.zeros((8, CH), F32)


def norm(x, gain, start):
    inverse = lax.rsqrt(jnp.mean(x * x, axis=-1, keepdims=True) + EPSILON)
    scaled = x * inverse
    normed = (scaled * gain).astype(BF16).astype(F32)
    keep = lax.broadcasted_iota(jnp.int32, (LINE, CH), 0) >= start
    return inverse, scaled, jnp.where(keep, normed, 0.0), keep


def conv(pad, masked, taps):
    total = None
    for t, moved in enumerate(shifts(pad, masked)):
        term = taps[t : t + 1, :] * moved
        total = term if total is None else total + term
    return total


def sigmoid(h):
    return 1.0 / (1.0 + jnp.exp(-h))


def forward_line(k, line, x, starts, gain_ref, taps_ref, mix_ref, pad):
    inverse, scaled, masked, keep = norm(x, gain_ref[k : k + 1, :], starts[k, line])
    hidden = conv(pad, masked, taps_ref[k])
    gate = sigmoid(hidden)
    active = (hidden * gate).astype(BF16)
    mixed = dot(active, mix_ref[k], 1, 0).astype(BF16).astype(F32)
    after = (x + mixed).astype(BF16)
    return inverse, scaled, masked, keep, hidden, gate, active, after


def backward_line(k, grad, state, gain_ref, taps_ref, mix_ref, pad, sums):
    inverse, scaled, masked, keep, hidden, gate, active = state
    gain = gain_ref[k : k + 1, :]
    taps = taps_ref[k]
    sums["mix"] = sums["mix"] + dot(active, grad, 0, 0)
    grad_act = dot(grad, mix_ref[k], 1, 1)
    grad_hidden = (grad_act * (gate * (1.0 + hidden * (1.0 - gate)))).astype(BF16).astype(F32)
    total = None
    for t, moved in enumerate(shifts(pad, grad_hidden)):
        u = t if t == 0 else (t + 1 if t % 2 else t - 1)
        term = taps[u : u + 1, :] * moved
        total = term if total is None else total + term
        part = jnp.sum((moved * masked).reshape(LINE // 8, 8, CH), axis=0)
        sums["taps"][u] = part if sums["taps"][u] is None else sums["taps"][u] + part
    cells = jnp.where(keep, total, 0.0).astype(BF16).astype(F32)
    part = jnp.sum((cells * scaled).reshape(LINE // 8, 8, CH), axis=0)
    sums["gain"] = part if sums["gain"] is None else sums["gain"] + part
    weighted = cells * gain
    moved = inverse * (weighted - scaled * jnp.mean(weighted * scaled, axis=-1, keepdims=True))
    return (grad.astype(F32) + moved).astype(BF16)


def new_sums():
    return {"mix": jnp.zeros((CH, CH), F32), "taps": [None] * TAPS, "gain": None}


def write_sums(ref, sums):
    ref[0:CH, :] = sums["mix"]
    rows = [jnp.sum(part, axis=0, keepdims=True) for part in sums["taps"]]
    rows.append(jnp.sum(sums["gain"], axis=0, keepdims=True))
    ref[CH:ROWS, :] = jnp.concatenate(rows, axis=0)


def prep_kernel(fields_ref, cot_ref, out_ref):
    me = lax.axis_index("line")
    for b in range(NL):
        out_ref[b, 0:Q, :] = fields_ref[0, b * Q : (b + 1) * Q, :]
        slot = jnp.bitwise_and(b + 2 * me, NL - 1)
        out_ref[pl.ds(slot, 1), Q : 2 * Q, :] = cot_ref[:, b * Q : (b + 1) * Q, :]


def forward_kernel(k, starts, in_ref, gain_ref, taps_ref, mix_ref, order_ref, out_ref, x_ref, h_ref, pad):
    clear(pad)
    received = in_ref[:, 0:Q, :].reshape(CELLS, CH)
    order = order_ref[k : k + 1, :]
    row = slot_row(order, 0 if k == 0 else -1)
    after = []
    for line in range(LINES):
        x = dot(picks(row, line), received, 1, 0)
        done = forward_line(k, line, x, starts, gain_ref, taps_ref, mix_ref, pad)
        x_ref[line] = x.astype(BF16)
        h_ref[line] = done[4]
        after.append(done[7])
    put(out_ref, 0, place(slot_row(order, 1), jnp.concatenate(after, axis=0)))


def turn_kernel(starts, in_ref, cot_ref, gain_ref, taps_ref, mix_ref, order_ref, out_ref, sum_ref, pad):
    k = 2
    clear(pad)
    received = in_ref[...].reshape(CELLS, CH)
    cot = cot_ref[:, Q : 2 * Q, :].reshape(CELLS, CH)
    order = order_ref[k : k + 1, :]
    row = slot_row(order, -1)
    sums = new_sums()
    after, grads = [], []
    for line in range(LINES):
        x = dot(picks(row, line), received, 1, 0)
        done = forward_line(k, line, x, starts, gain_ref, taps_ref, mix_ref, pad)
        after.append(done[7])
        grad = dot(picks(order, line), cot, 1, 0).astype(BF16)
        grads.append(backward_line(k, grad, done[:7], gain_ref, taps_ref, mix_ref, pad, sums))
    put(out_ref, 0, place(order, jnp.concatenate(after, axis=0)))
    put(out_ref, Q, place(row, jnp.concatenate(grads, axis=0)))
    write_sums(sum_ref, sums)


def rank_at(zone, core):
    me = lax.axis_index("line")
    chip = jnp.bitwise_and(lax.shift_right_logical(me, 1) + zone, CHIPS - 1)
    return chip * 2 + jnp.bitwise_xor(jnp.bitwise_and(me, 1), core)


def share_out(sum_refs, small_ref, keep_ref, send_ref):
    for r in range(NL):
        for k, ref in enumerate(sum_refs):
            small_ref[r, 2 * k : 2 * k + 2, :] = ref[CH + 2 * r : CH + 2 * r + 2, :]
        small_ref[r, 6:8, :] = jnp.zeros((2, CH), F32)
    for core, out in ((0, keep_ref), (1, send_ref)):
        for zone in range(CHIPS):
            r = rank_at(zone, core)
            for k, ref in enumerate(sum_refs):
                out[zone, k * 16 : (k + 1) * 16, :] = ref[pl.ds(pl.multiple_of(r * 16, 16), 16), :]
            out[zone, 48:SHARE, :] = small_ref[pl.ds(r, 1), :, :].reshape(8, CH)


def finish_kernel(own_ref, other_ref, mix_ref, taps_ref, gain_ref, tail_ref):
    for core, ref in ((0, own_ref), (1, other_ref)):
        for zone in range(CHIPS):
            r = rank_at(CHIPS - zone, core)
            for k in range(3):
                mix_ref[k, pl.ds(pl.multiple_of(r * 16, 16), 16), :] = ref[zone, k * 16 : (k + 1) * 16, :]
            tail_ref[pl.ds(r, 1), :, :] = ref[zone, 48:SHARE, :].reshape(1, 8, CH)
    for k in range(3):
        for r in range(NL):
            pair = tail_ref[r, 2 * k : 2 * k + 2, :]
            if r < NL - 1:
                taps_ref[k, 2 * r : 2 * r + 2, :] = pair
            else:
                taps_ref[k, 2 * r : 2 * r + 1, :] = pair[0:1]
                gain_ref[k : k + 1, :] = pair[1:2]


def backward_kernel(k, starts, in_ref, x_ref, h_ref, gain_ref, taps_ref, mix_ref, order_ref, *rest):
    if k == 1:
        out_ref, sum_ref, imitated_ref, pad = rest
        me = lax.axis_index("line")
        for b in range(NL):
            slot = jnp.bitwise_and(b + 2 * me, NL - 1)
            imitated_ref[:, b * Q : (b + 1) * Q, :] = in_ref[pl.ds(slot, 1), 0:Q, :]
        received = in_ref[:, Q : 2 * Q, :].reshape(CELLS, CH)
    else:
        sum1_ref, sum2_ref, out_ref, keep_ref, send_ref, pad, sum_ref, small_ref = rest
        received = in_ref[...].reshape(CELLS, CH)
    clear(pad)
    order = order_ref[k : k + 1, :]
    row = slot_row(order, 1)
    sums = new_sums()
    grads = []
    for line in range(LINES):
        grad = dot(picks(row, line), received, 1, 0).astype(BF16)
        x = x_ref[line].astype(F32)
        hidden = h_ref[line]
        inverse, scaled, masked, keep = norm(x, gain_ref[k : k + 1, :], starts[k, line])
        gate = sigmoid(hidden)
        active = (hidden * gate).astype(BF16)
        state = (inverse, scaled, masked, keep, hidden, gate, active)
        grads.append(backward_line(k, grad, state, gain_ref, taps_ref, mix_ref, pad, sums))
    put(out_ref, 0, place(slot_row(order, -1 if k else 0), jnp.concatenate(grads, axis=0)))
    write_sums(sum_ref, sums)
    if k == 0:
        share_out((sum_ref, sum1_ref, sum2_ref), small_ref, keep_ref, send_ref)


def call(kernel, outs, name, n_in, scratch=()):
    smem = pl.BlockSpec(memory_space=pltpu.SMEM)
    vmem = pl.BlockSpec(memory_space=pltpu.VMEM)
    return pl.pallas_call(
        kernel,
        out_shape=outs,
        in_specs=([smem] if n_in > 2 else [vmem]) + [vmem] * (n_in - 1),
        out_specs=[vmem] * len(outs),
        scratch_shapes=[pltpu.VMEM((LINE + 16, CH), F32)] * (n_in > 2)
        + [pltpu.VMEM(dims, F32) for dims in scratch],
        name=name,
        compiler_params=pltpu.CompilerParams(vmem_limit_bytes=VMEM_GRANT),
    )


def shape(*dims, dtype=BF16):
    return jax.ShapeDtypeStruct(dims, dtype)


def hop(axis, bit, values):
    size = lax.axis_size(axis)
    return lax.ppermute(values, axis, [(i, i ^ bit) for i in range(size)])


def step(axis, distance, values):
    size = lax.axis_size(axis)
    return lax.ppermute(values, axis, [(i, (i + distance) % size) for i in range(size)])


def exchange(blocks):
    return lax.all_to_all(blocks, "line", split_axis=0, concat_axis=0, tiled=True)


def body(fields, cotangent, norm_gain, kernel, mix_weight, line_order, line_starts):
    dp_size = lax.axis_size("dp")
    weights = (norm_gain, kernel, mix_weight, line_order)
    state = (shape(LINES, LINE, CH), shape(LINES, LINE, CH, dtype=F32))
    sums = shape(ROWS, CH, dtype=F32)
    blocks = shape(NL, Q, CH)
    (packed,) = call(prep_kernel, (shape(NL, 2 * Q, CH),), "prep", 2)(fields, cotangent)
    first = exchange(packed)
    moved, x0, h0 = call(functools.partial(forward_kernel, 0), (blocks, *state), "fwd0", 6)(
        line_starts, first, *weights
    )
    moved, x1, h1 = call(functools.partial(forward_kernel, 1), (blocks, *state), "fwd1", 6)(
        line_starts, exchange(moved), *weights
    )
    moved, sums2 = call(turn_kernel, (shape(NL, 2 * Q, CH), sums), "turn", 7)(
        line_starts, exchange(moved), first, *weights
    )
    moved, sums1, imitated = call(
        functools.partial(backward_kernel, 1), (blocks, sums, shape(1, CELLS, CH)), "bwd1", 8
    )(line_starts, exchange(moved), x1, h1, *weights)
    share = shape(CHIPS, SHARE, CH, dtype=F32)
    moved, keep, send = call(
        functools.partial(backward_kernel, 0),
        (blocks, share, share),
        "bwd0",
        10,
        scratch=((ROWS, CH), (NL, 8, CH)),
    )(line_starts, exchange(moved), x0, h0, *weights, sums1, sums2)
    field_grad = exchange(moved).reshape(1, CELLS, CH)
    grad_scale = float(dp_size * NL * CELLS) ** (-0.5)
    part = keep + hop("line", 1, send)
    part = part[0] + sum(step("line", 2 * zone, part[zone]) for zone in range(1, CHIPS))
    bit = 1
    while bit < dp_size:
        part = part + hop("dp", bit, part)
        bit *= 2
    part = part * grad_scale
    own = jnp.stack([part] + [step("line", 2 * zone, part) for zone in range(1, CHIPS)])
    mix_grad, kernel_grad, gain_grad = call(
        finish_kernel,
        (shape(3, CH, CH, dtype=F32), shape(3, TAPS, CH, dtype=F32), shape(3, CH, dtype=F32)),
        "finish",
        2,
        scratch=((NL, 8, CH),),
    )(own, hop("line", 1, own))
    return imitated, field_grad, mix_grad, kernel_grad, gain_grad


def solution(mesh):
    in_specs = (
        P("dp", "line", None),
        P("dp", "line", None),
        P(),
        P(),
        P(),
        P(None, "line"),
        P(None, "line"),
    )
    out_specs = (P("dp", "line", None), P("dp", "line", None), P(), P(), P())
    return jax.shard_map(body, mesh=mesh, in_specs=in_specs, out_specs=out_specs, check_vma=False)
```

```python
import functools

import jax
import jax.numpy as jnp
from jax import lax
from jax.experimental import pallas as pl
from jax.experimental.pallas import tpu as pltpu
from jax.sharding import PartitionSpec as P

LINE = 128
CH = 128
TAPS = 15
CELLS = 512
NL = 8
CHIPS = NL // 2
Q = CELLS // NL
HALF = CELLS // 2
LINES = CELLS // LINE
EPSILON = 1e-06
OFFSETS = [0] + [s * 2**level for level in range(7) for s in (-1, 1)]
F32 = jnp.float32
BF16 = jnp.bfloat16
I32 = jnp.int32
ROWS = LINE + TAPS + 1
EXTRA = 48
SHARE = 56
VMEM_GRANT = 12 * 2**20


def dot(a, b, ca, cb):
    return lax.dot_general(a, b, (((ca,), (cb,)), ((), ())), preferred_element_type=F32)


def place_of():
    me = lax.axis_index("line")
    return lax.shift_right_logical(me, 1), jnp.bitwise_and(me, 1)


def wrap(index):
    return jnp.bitwise_and(index, CHIPS - 1)


def block_row(order, gathered):
    home = lax.shift_right_logical(order, 6)
    within = jnp.bitwise_and(order, Q - 1)
    odd = jnp.bitwise_and(home, 1)
    chip = lax.shift_right_logical(home, 1)
    if gathered:
        zone, core = place_of()
        odd = jnp.bitwise_xor(odd, core)
        chip = wrap(zone - chip + CHIPS)
    return odd * HALF + chip * Q + within


def picks(row, line):
    part = row[:, line * LINE : (line + 1) * LINE]
    wanted = jnp.transpose(jnp.broadcast_to(part, (LINE, LINE)))
    lanes = lax.broadcasted_iota(I32, (LINE, LINE), 1)
    return jnp.concatenate(
        [jnp.where(wanted == lanes + c * LINE, 1.0, 0.0).astype(BF16) for c in range(LINES)],
        axis=1,
    )


def place(row, values, rows):
    hot = jnp.where(jnp.broadcast_to(row, (LINE, CELLS)) == rows, 1.0, 0.0).astype(BF16)
    return dot(hot, values, 1, 0).astype(BF16)


def put_next(row, values, m, sign, same_ref, swap_ref):
    _, core = place_of()
    for c in range(LINES):
        rows = lax.broadcasted_iota(I32, (LINE, CELLS), 0) + c * LINE
        placed = place(row, values, rows)
        for half in range(2):
            h = (c * 2 + half) % CHIPS
            block = placed[half * Q : (half + 1) * Q]
            if c < LINES // 2:
                same_ref[wrap(m + sign * h + CHIPS), h] = block
            else:
                at = m + h + core if sign > 0 else m - h - 1 + core + CHIPS
                swap_ref[wrap(at), h] = block


def put_home(row, values, m, own_ref, swap_ref):
    zone, core = place_of()
    step = lax.broadcasted_iota(I32, (LINE, CELLS), 0)
    mine = (core * CHIPS + zone) * Q
    other = ((1 - core) * CHIPS + zone) * Q - Q
    placed = place(row, values, step + jnp.where(step < Q, mine, other))
    own_ref[m] = placed[:Q]
    swap_ref[m] = placed[Q:]


def shifts(pad, values):
    pad[8 : 8 + LINE, :] = values
    for offset in OFFSETS:
        if offset == 0:
            yield values
        elif abs(offset) < 8:
            yield pad[8 + offset : 8 + offset + LINE, :]
        elif offset > 0:
            yield jnp.concatenate([values[offset:], jnp.zeros((offset, CH), F32)], axis=0)
        else:
            yield jnp.concatenate([jnp.zeros((-offset, CH), F32), values[:offset]], axis=0)


def clear(pad):
    pad[0:8, :] = jnp.zeros((8, CH), F32)
    pad[8 + LINE : 16 + LINE, :] = jnp.zeros((8, CH), F32)


def norm(x, gain, start):
    inverse = lax.rsqrt(jnp.mean(x * x, axis=-1, keepdims=True) + EPSILON)
    scaled = x * inverse
    normed = (scaled * gain).astype(BF16).astype(F32)
    keep = lax.broadcasted_iota(I32, (LINE, CH), 0).astype(F32) >= start
    return inverse, scaled, jnp.where(keep, normed, 0.0), keep


def conv(pad, masked, taps):
    total = None
    for t, moved in enumerate(shifts(pad, masked)):
        term = taps[t : t + 1, :] * moved
        total = term if total is None else total + term
    return total


def sigmoid(h):
    return 1.0 / (1.0 + jnp.exp(-h))


def forward_line(k, x, start, gain_ref, taps_ref, mix_ref, pad):
    inverse, scaled, masked, keep = norm(x, gain_ref[k : k + 1, :], start)
    hidden = conv(pad, masked, taps_ref[k])
    gate = sigmoid(hidden)
    active = (hidden * gate).astype(BF16)
    mixed = dot(active, mix_ref[k], 1, 0).astype(BF16).astype(F32)
    after = (x + mixed).astype(BF16)
    return (inverse, scaled, masked, keep, hidden, gate, active), after


def backward_line(k, grad, state, gain_ref, taps_ref, mix_ref, pad, sums):
    inverse, scaled, masked, keep, hidden, gate, active = state
    gain = gain_ref[k : k + 1, :]
    taps = taps_ref[k]
    sums["active"].append(active)
    sums["grad"].append(grad)
    grad_act = dot(grad, mix_ref[k], 1, 1)
    grad_hidden = (grad_act * (gate * (1.0 + hidden * (1.0 - gate)))).astype(BF16).astype(F32)
    total = None
    for t, moved in enumerate(shifts(pad, grad_hidden)):
        u = t if t == 0 else (t + 1 if t % 2 else t - 1)
        term = taps[u : u + 1, :] * moved
        total = term if total is None else total + term
        part = jnp.sum((moved * masked).reshape(LINE // 8, 8, CH), axis=0)
        sums["rows"][u] = part if sums["rows"][u] is None else sums["rows"][u] + part
    cells = jnp.where(keep, total, 0.0).astype(BF16).astype(F32)
    part = jnp.sum((cells * scaled).reshape(LINE // 8, 8, CH), axis=0)
    sums["rows"][TAPS] = part if sums["rows"][TAPS] is None else sums["rows"][TAPS] + part
    weighted = cells * gain
    moved = inverse * (weighted - scaled * jnp.mean(weighted * scaled, axis=-1, keepdims=True))
    return (grad.astype(F32) + moved).astype(BF16)


def new_sums():
    return {"active": [], "grad": [], "rows": [None] * (TAPS + 1)}


def add_sums(sum_ref, rows_ref, sums):
    active = jnp.concatenate(sums["active"], axis=0)
    sum_ref[0:CH, :] += dot(active, jnp.concatenate(sums["grad"], axis=0), 0, 0)
    for t, part in enumerate(sums["rows"]):
        rows_ref[t] += part


def start_sums(sum_ref, rows_ref):
    sum_ref[...] = jnp.zeros_like(sum_ref)
    rows_ref[...] = jnp.zeros_like(rows_ref)


def end_sums(sum_ref, rows_ref):
    sum_ref[CH:ROWS, :] = jnp.sum(rows_ref[...], axis=1)


def prep_kernel(starts, fields_ref, cot_ref, order_ref, keep_ref, keep_cot_ref, send_ref, extra_ref):
    _, core = place_of()
    for m in range(CHIPS):
        here = pl.ds(pl.multiple_of((2 * m + core) * Q, Q), Q)
        there = pl.ds(pl.multiple_of((2 * m + 1 - core) * Q, Q), Q)
        keep_ref[m] = fields_ref[0, here, :]
        keep_cot_ref[m] = cot_ref[0, here, :]
        send_ref[m] = fields_ref[0, there, :]
        send_ref[CHIPS + m] = cot_ref[0, there, :]
    rows = []
    for k in range(3):
        order = order_ref[k : k + 1, :]
        for part in (lax.shift_right_logical(order, 1), jnp.bitwise_and(order, 1)):
            rows += [part[:, c * LINE : (c + 1) * LINE].astype(F32) for c in range(LINES)]
    for k in range(3):
        rows += [jnp.full((1, CH), starts[k, line], I32).astype(F32) for line in range(LINES)]
    rows.append(jnp.zeros((EXTRA - len(rows), CH), F32))
    extra_ref[...] = jnp.concatenate(rows, axis=0).astype(BF16)


def read_tables(pieces, order_ref, starts_ref):
    zone, _ = place_of()
    for back, ref in enumerate(pieces):
        m = wrap(zone - back + CHIPS)
        extra = ref[CELLS : CELLS + EXTRA, :].astype(F32)
        for k in range(3):
            for c in range(LINES):
                high = extra[8 * k + c : 8 * k + c + 1]
                low = extra[8 * k + 4 + c : 8 * k + 5 + c]
                order_ref[k, m, :, c * LINE : (c + 1) * LINE] = (2.0 * high + low).astype(I32)
            starts_ref[k, m] = extra[24 + 4 * k : 28 + 4 * k]


def gathered_rows(pieces, m, k):
    zone, core = place_of()
    rows = []
    for odd in range(2):
        for back, ref in enumerate(pieces):
            home = 2 * (zone - back) + jnp.bitwise_xor(core, odd)
            block = wrap(m - (k // 2) * home + NL)
            rows.append(ref[pl.ds(pl.multiple_of(odd * HALF + block * Q, Q), Q), :])
    return jnp.concatenate(rows, axis=0)


def moved_rows(same_ref, swap_ref, m):
    return jnp.concatenate([same_ref[m].reshape(HALF, CH), swap_ref[m].reshape(HALF, CH)], axis=0)


def forward_kernel(k, *refs):
    if k == 0:
        pieces, refs = refs[:CHIPS], refs[CHIPS:]
        gain_ref, taps_ref, mix_ref, order_ref, starts_ref, same_ref, swap_ref, x_ref, h_ref, pad = refs
        read_tables(pieces, order_ref, starts_ref)
    else:
        (in_ref, in_swap_ref, gain_ref, taps_ref, mix_ref, order_ref, starts_ref) = refs[:7]
        same_ref, swap_ref, x_ref, h_ref, pad = refs[7:]
    clear(pad)

    def holder(m, carry):
        received = gathered_rows(pieces, m, k) if k == 0 else moved_rows(in_ref, in_swap_ref, m)
        order = order_ref[k, m]
        row = block_row(order, k == 0)
        after = []
        for line in range(LINES):
            x = dot(picks(row, line), received, 1, 0)
            state, new = forward_line(
                k, x, starts_ref[k, m, line : line + 1, :], gain_ref, taps_ref, mix_ref, pad
            )
            x_ref[m, line] = x.astype(BF16)
            h_ref[m, line] = state[4]
            after.append(new)
        put_next(block_row(order, False), jnp.concatenate(after, axis=0), m, 1, same_ref, swap_ref)
        return carry

    lax.fori_loop(0, CHIPS, holder, 0)


def turn_kernel(*refs):
    k = 2
    in_ref, in_swap_ref = refs[:2]
    pieces = refs[2 : 2 + CHIPS]
    gain_ref, taps_ref, mix_ref, order_ref, starts_ref = refs[2 + CHIPS : 7 + CHIPS]
    same_ref, swap_ref, own_ref, home_ref, sum_ref, pad, rows_ref = refs[7 + CHIPS :]
    clear(pad)
    start_sums(sum_ref, rows_ref)

    def holder(m, carry):
        received = moved_rows(in_ref, in_swap_ref, m)
        cot = gathered_rows(pieces, m, k)
        order = order_ref[k, m]
        row = block_row(order, False)
        cot_row = block_row(order, True)
        sums = new_sums()
        after, grads = [], []
        for line in range(LINES):
            x = dot(picks(row, line), received, 1, 0)
            state, new = forward_line(
                k, x, starts_ref[k, m, line : line + 1, :], gain_ref, taps_ref, mix_ref, pad
            )
            after.append(new)
            grad = dot(picks(cot_row, line), cot, 1, 0).astype(BF16)
            grads.append(backward_line(k, grad, state, gain_ref, taps_ref, mix_ref, pad, sums))
        put_home(row, jnp.concatenate(after, axis=0), m, own_ref, home_ref)
        put_next(row, jnp.concatenate(grads, axis=0), m, -1, same_ref, swap_ref)
        add_sums(sum_ref, rows_ref, sums)
        return carry

    lax.fori_loop(0, CHIPS, holder, 0)
    end_sums(sum_ref, rows_ref)


def share_out(sum_refs, small_ref, keep_ref, send_ref):
    zone, core = place_of()
    for r in range(NL):
        for k, ref in enumerate(sum_refs):
            small_ref[r, 2 * k : 2 * k + 2, :] = ref[CH + 2 * r : CH + 2 * r + 2, :]
        small_ref[r, 6:8, :] = jnp.zeros((2, CH), F32)
    for r, out in ((2 * zone + core, keep_ref), (2 * zone + 1 - core, send_ref)):
        for k, ref in enumerate(sum_refs):
            out[k * 16 : (k + 1) * 16, :] = ref[pl.ds(pl.multiple_of(r * 16, 16), 16), :]
        out[48:SHARE, :] = small_ref[r]


def backward_kernel(k, *refs):
    in_ref, in_swap_ref, x_ref, h_ref, gain_ref, taps_ref, mix_ref, order_ref, starts_ref = refs[:9]
    if k == 1:
        own_ref, home_ref, same_ref, swap_ref, sum_ref, imitated_ref, pad, rows_ref = refs[9:]
        zone, core = place_of()
        for m in range(CHIPS):
            for ref, first in ((own_ref, 2 * m - core), (home_ref, 2 * m + 1 - 3 * core)):
                b = jnp.bitwise_and(first - 4 * zone + 4 * NL, NL - 1)
                imitated_ref[0, pl.ds(pl.multiple_of(b * Q, Q), Q), :] = ref[m]
    else:
        sum1_ref, sum2_ref, own_ref, home_ref, keep_ref, send_ref, pad, rows_ref, sum_ref, small_ref = refs[9:]
    clear(pad)
    start_sums(sum_ref, rows_ref)

    def holder(m, carry):
        received = moved_rows(in_ref, in_swap_ref, m)
        row = block_row(order_ref[k, m], False)
        sums = new_sums()
        grads = []
        for line in range(LINES):
            grad = dot(picks(row, line), received, 1, 0).astype(BF16)
            hidden = h_ref[m, line]
            inverse, scaled, masked, keep = norm(
                x_ref[m, line].astype(F32), gain_ref[k : k + 1, :], starts_ref[k, m, line : line + 1, :]
            )
            gate = sigmoid(hidden)
            state = (inverse, scaled, masked, keep, hidden, gate, (hidden * gate).astype(BF16))
            grads.append(backward_line(k, grad, state, gain_ref, taps_ref, mix_ref, pad, sums))
        if k == 1:
            put_next(row, jnp.concatenate(grads, axis=0), m, -1, same_ref, swap_ref)
        else:
            put_home(row, jnp.concatenate(grads, axis=0), m, own_ref, home_ref)
        add_sums(sum_ref, rows_ref, sums)
        return carry

    lax.fori_loop(0, CHIPS, holder, 0)
    end_sums(sum_ref, rows_ref)
    if k == 0:
        share_out((sum_ref, sum1_ref, sum2_ref), small_ref, keep_ref, send_ref)


def finish_kernel(own_ref, other_ref, grad_ref, home_ref, mix_ref, taps_ref, gain_ref, out_ref, tail_ref):
    zone, core = place_of()
    for m in range(CHIPS):
        for ref, b in ((grad_ref, 2 * m + core), (home_ref, 2 * m + 1 - core)):
            out_ref[0, pl.ds(pl.multiple_of(b * Q, Q), Q), :] = ref[m]
    for ref, side in ((own_ref, core), (other_ref, 1 - core)):
        for back in range(CHIPS):
            r = 2 * wrap(zone - back + CHIPS) + side
            for k in range(3):
                mix_ref[k, pl.ds(pl.multiple_of(r * 16, 16), 16), :] = ref[back, k * 16 : (k + 1) * 16, :]
            tail_ref[r] = ref[back, 48:SHARE, :]
    for k in range(3):
        for r in range(NL):
            pair = tail_ref[r, 2 * k : 2 * k + 2, :]
            if r < NL - 1:
                taps_ref[k, 2 * r : 2 * r + 2, :] = pair
            else:
                taps_ref[k, 2 * r : 2 * r + 1, :] = pair[0:1]
                gain_ref[k : k + 1, :] = pair[1:2]


def call(kernel, outs, name, n_in, scratch=(), scalars=0):
    smem = pl.BlockSpec(memory_space=pltpu.SMEM)
    vmem = pl.BlockSpec(memory_space=pltpu.VMEM)
    return pl.pallas_call(
        kernel,
        out_shape=outs,
        in_specs=[smem] * scalars + [vmem] * (n_in - scalars),
        out_specs=[vmem] * len(outs),
        scratch_shapes=[pltpu.VMEM(dims, F32) for dims in scratch],
        name=name,
        compiler_params=pltpu.CompilerParams(vmem_limit_bytes=VMEM_GRANT),
    )


def shape(*dims, dtype=BF16):
    return jax.ShapeDtypeStruct(dims, dtype)


def swap(values):
    return lax.ppermute(values, "line", [(i, i ^ 1) for i in range(NL)])


def from_chips(values):
    got = {
        back: lax.ppermute(values, "line", [(i, (i + 2 * back) % NL) for i in range(NL)])
        for back in (2, 1, 3)
    }
    return [values, got[1], got[2], got[3]]


def sum_over_dp(part):
    size = lax.axis_size("dp")
    stride = 1
    while stride < size:
        ring = 4 if size % (stride * 4) == 0 else 2
        got = [part]
        for turn in range(1, ring):
            pairs = []
            for i in range(size):
                at = i // stride % ring
                pairs.append((i, i + ((at + turn) % ring - at) * stride))
            got.append(lax.ppermute(part, "dp", pairs))
        part = sum(got[1:], got[0])
        stride *= ring
    return part


def body(fields, cotangent, norm_gain, kernel, mix_weight, line_order, line_starts):
    dp_size = lax.axis_size("dp")
    weights = (norm_gain, kernel, mix_weight)
    quarter = shape(CHIPS, Q, CH)
    moving = shape(CHIPS, CHIPS, Q, CH)
    tables = (shape(3, CHIPS, 1, CELLS, dtype=I32), shape(3, CHIPS, LINES, CH, dtype=F32))
    state = (shape(CHIPS, LINES, LINE, CH), shape(CHIPS, LINES, LINE, CH, dtype=F32))
    sums = shape(ROWS, CH, dtype=F32)
    pad = (LINE + 16, CH)
    parts = (TAPS + 1, 8, CH)

    keep, keep_cot, send, extra = call(
        prep_kernel, (quarter, quarter, shape(NL, Q, CH), shape(EXTRA, CH)), "prep", 4, scalars=1
    )(line_starts, fields, cotangent, line_order)
    got = swap(send)
    piece = jnp.concatenate([keep.reshape(HALF, CH), got[:CHIPS].reshape(HALF, CH), extra])
    piece_cot = jnp.concatenate([keep_cot.reshape(HALF, CH), got[CHIPS:].reshape(HALF, CH)])
    pieces = from_chips(piece)
    pieces_cot = from_chips(piece_cot)
    order, starts, same, moved, x0, h0 = call(
        functools.partial(forward_kernel, 0), (*tables, moving, moving, *state), "fwd0", 7, scratch=(pad,)
    )(*pieces, *weights)
    given = (*weights, order, starts)
    same, moved, x1, h1 = call(
        functools.partial(forward_kernel, 1), (moving, moving, *state), "fwd1", 7, scratch=(pad,)
    )(same, swap(moved), *given)
    same, moved, own, home, sums2 = call(
        turn_kernel, (moving, moving, quarter, quarter, sums), "turn", 11, scratch=(pad, parts)
    )(same, swap(moved), *pieces_cot, *given)
    same, moved, sums1, imitated = call(
        functools.partial(backward_kernel, 1),
        (moving, moving, sums, shape(1, CELLS, CH)),
        "bwd1",
        11,
        scratch=(pad, parts),
    )(same, swap(moved), x1, h1, *given, own, swap(home))
    share = shape(SHARE, CH, dtype=F32)
    own, home, keep, send = call(
        functools.partial(backward_kernel, 0),
        (quarter, quarter, share, share),
        "bwd0",
        11,
        scratch=(pad, parts, (ROWS, CH), (NL, 8, CH)),
    )(same, swap(moved), x0, h0, *given, sums1, sums2)
    grad_scale = float(dp_size * NL * CELLS) ** (-0.5)
    part = sum_over_dp(keep + swap(send)) * grad_scale
    shares = jnp.stack(from_chips(part))
    mix_grad, kernel_grad, gain_grad, field_grad = call(
        finish_kernel,
        (
            shape(3, CH, CH, dtype=F32),
            shape(3, TAPS, CH, dtype=F32),
            shape(3, CH, dtype=F32),
            shape(1, CELLS, CH),
        ),
        "finish",
        4,
        scratch=((NL, 8, CH),),
    )(shares, swap(shares), own, swap(home))
    return imitated, field_grad, mix_grad, kernel_grad, gain_grad


def solution(mesh):
    in_specs = (
        P("dp", "line", None),
        P("dp", "line", None),
        P(),
        P(),
        P(),
        P(None, "line"),
        P(None, "line"),
    )
    out_specs = (P("dp", "line", None), P("dp", "line", None), P(), P(), P())
    return jax.shard_map(body, mesh=mesh, in_specs=in_specs, out_specs=out_specs, check_vma=False)
```

```python
import functools

import jax
import jax.numpy as jnp
from jax import lax
from jax.experimental import pallas as pl
from jax.experimental.pallas import tpu as pltpu
from jax.sharding import PartitionSpec as P


LINE = 128
CH = 128
TAPS = 15
CELLS = 512
NL = 8
CHIPS = NL // 2
RING = 4
Q = CELLS // NL
HALF = CELLS // 2
LINES = CELLS // LINE
EPSILON = 1e-06
OFFSETS = [0] + [s * 2**level for level in range(7) for s in (-1, 1)]
F32 = jnp.float32
BF16 = jnp.bfloat16
I32 = jnp.int32
ROWS = LINE + TAPS + 1
EXTRA = 48
SHARE = 56
VMEM_GRANT = 12 * 2**20


def dot(a, b, ca, cb):
    return lax.dot_general(a, b, (((ca,), (cb,)), ((), ())), preferred_element_type=F32)


def place_of():
    me = lax.axis_index("line")
    return lax.shift_right_logical(me, 1), jnp.bitwise_and(me, 1)


def wrap(index):
    return jnp.bitwise_and(index, CHIPS - 1)


def block_row(order, gathered):
    home = lax.shift_right_logical(order, 6)
    within = jnp.bitwise_and(order, Q - 1)
    odd = jnp.bitwise_and(home, 1)
    chip = lax.shift_right_logical(home, 1)
    if gathered:
        zone, core = place_of()
        odd = jnp.bitwise_xor(odd, core)
        chip = wrap(zone - chip + CHIPS)
    return odd * HALF + chip * Q + within


def picks(row, line):
    part = row[:, line * LINE : (line + 1) * LINE]
    wanted = jnp.transpose(jnp.broadcast_to(part, (LINE, LINE)))
    lanes = lax.broadcasted_iota(I32, (LINE, LINE), 1)
    return jnp.concatenate(
        [jnp.where(wanted == lanes + c * LINE, 1.0, 0.0).astype(BF16) for c in range(LINES)],
        axis=1,
    )


def place(row, values, rows):
    hot = jnp.where(jnp.broadcast_to(row, (LINE, CELLS)) == rows, 1.0, 0.0).astype(BF16)
    return dot(hot, values, 1, 0).astype(BF16)


def put_next(row, values, m, sign, same_ref, swap_ref):
    _, core = place_of()
    for c in range(LINES):
        rows = lax.broadcasted_iota(I32, (LINE, CELLS), 0) + c * LINE
        placed = place(row, values, rows)
        for half in range(2):
            h = (c * 2 + half) % CHIPS
            block = placed[half * Q : (half + 1) * Q]
            if c < LINES // 2:
                same_ref[wrap(m + sign * h + CHIPS), h] = block
            else:
                at = m + h + core if sign > 0 else m - h - 1 + core + CHIPS
                swap_ref[wrap(at), h] = block


def put_home(row, values, m, own_ref, swap_ref):
    zone, core = place_of()
    step = lax.broadcasted_iota(I32, (LINE, CELLS), 0)
    mine = (core * CHIPS + zone) * Q
    other = ((1 - core) * CHIPS + zone) * Q - Q
    placed = place(row, values, step + jnp.where(step < Q, mine, other))
    own_ref[m] = placed[:Q]
    swap_ref[m] = placed[Q:]


def shifts(pad, values):
    pad[8 : 8 + LINE, :] = values
    for offset in OFFSETS:
        if offset == 0:
            yield 0, values
        elif abs(offset) < 8:
            yield 0, pad[8 + offset : 8 + offset + LINE, :]
        elif offset > 0:
            yield 0, values[offset:]
        else:
            yield -offset, values[:offset]


def accumulate(total, first, rows):
    size = rows.shape[0]
    pieces = [total[:first]] if first else []
    pieces.append(total[first : first + size] + rows)
    if first + size < LINE:
        pieces.append(total[first + size :])
    return jnp.concatenate(pieces, axis=0) if len(pieces) > 1 else pieces[0]


def clear(pads):
    for line in range(LINES):
        pads[line, 0:8, :] = jnp.zeros((8, CH), F32)
        pads[line, 8 + LINE : 16 + LINE, :] = jnp.zeros((8, CH), F32)


def norm(x, gain, start):
    inverse = lax.rsqrt(jnp.mean(x * x, axis=-1, keepdims=True) + EPSILON)
    scaled = x * inverse
    normed = (scaled * gain).astype(BF16).astype(F32)
    keep = lax.broadcasted_iota(I32, (LINE, CH), 0).astype(F32) >= start
    return inverse, scaled, jnp.where(keep, normed, 0.0), keep


def conv(pad, masked, taps):
    total = None
    for t, (first, moved) in enumerate(shifts(pad, masked)):
        term = taps[t : t + 1, :] * moved
        total = term if total is None else accumulate(total, first, term)
    return total


def sigmoid(h):
    return 1.0 / (1.0 + jnp.exp(-h))


def forward_line(k, x, start, gain_ref, taps_ref, mix_ref, pad):
    inverse, scaled, masked, keep = norm(x, gain_ref[k : k + 1, :], start)
    hidden = conv(pad, masked, taps_ref[k])
    gate = sigmoid(hidden)
    active = (hidden * gate).astype(BF16)
    mixed = dot(active, mix_ref[k], 1, 0).astype(BF16).astype(F32)
    after = (x + mixed).astype(BF16)
    return (inverse, scaled, masked, keep, hidden, gate, active), after


def backward_line(k, grad, state, gain_ref, taps_ref, mix_ref, pad, sums):
    inverse, scaled, masked, keep, hidden, gate, active = state
    gain = gain_ref[k : k + 1, :]
    taps = taps_ref[k]
    sums["active"].append(active)
    sums["grad"].append(grad)
    grad_act = dot(grad, mix_ref[k], 1, 1)
    grad_hidden = (grad_act * (gate * (1.0 + hidden * (1.0 - gate)))).astype(BF16).astype(F32)
    total = None
    for t, (first, moved) in enumerate(shifts(pad, grad_hidden)):
        u = t if t == 0 else (t + 1 if t % 2 else t - 1)
        size = moved.shape[0]
        term = taps[u : u + 1, :] * moved
        total = term if total is None else accumulate(total, first, term)
        part = jnp.sum((moved * masked[first : first + size]).reshape(size // 8, 8, CH), axis=0)
        sums["rows"][u] = part if sums["rows"][u] is None else sums["rows"][u] + part
    cells = jnp.where(keep, total, 0.0).astype(BF16).astype(F32)
    part = jnp.sum((cells * scaled).reshape(LINE // 8, 8, CH), axis=0)
    sums["rows"][TAPS] = part if sums["rows"][TAPS] is None else sums["rows"][TAPS] + part
    weighted = cells * gain
    moved = inverse * (weighted - scaled * jnp.mean(weighted * scaled, axis=-1, keepdims=True))
    return (grad.astype(F32) + moved).astype(BF16)


def new_sums():
    return {"active": [], "grad": [], "rows": [None] * (TAPS + 1)}


def add_sums(sum_ref, rows_ref, sums):
    active = jnp.concatenate(sums["active"], axis=0)
    sum_ref[0:CH, :] += dot(active, jnp.concatenate(sums["grad"], axis=0), 0, 0)
    for t, part in enumerate(sums["rows"]):
        rows_ref[t] += part


def start_sums(sum_ref, rows_ref):
    sum_ref[...] = jnp.zeros_like(sum_ref)
    rows_ref[...] = jnp.zeros_like(rows_ref)


def end_sums(sum_ref, rows_ref):
    sum_ref[CH:ROWS, :] = jnp.sum(rows_ref[...], axis=1)


def prep_kernel(fields_ref, cot_ref, table_ref, begin_ref, keep_ref, keep_cot_ref, send_ref, extra_ref, order_ref, starts_ref, sem):
    _, core = place_of()
    copies = [
        pltpu.make_async_copy(table_ref, order_ref, sem.at[0]),
        pltpu.make_async_copy(begin_ref, starts_ref, sem.at[1]),
    ]
    for m in range(CHIPS):
        here = pl.ds(pl.multiple_of((2 * m + core) * Q, Q), Q)
        there = pl.ds(pl.multiple_of((2 * m + 1 - core) * Q, Q), Q)
        for source, own, first in ((fields_ref, keep_ref, 0), (cot_ref, keep_cot_ref, CHIPS)):
            for rows, target in ((here, own.at[m]), (there, send_ref.at[first + m])):
                copies.append(pltpu.make_async_copy(source.at[0, rows, :], target, sem.at[len(copies)]))
    for copy in copies:
        copy.start()
    for copy in copies[:2]:
        copy.wait()
    rows = []
    for k in range(3):
        order = order_ref[k : k + 1, :]
        for part in (lax.shift_right_logical(order, 1), jnp.bitwise_and(order, 1)):
            rows += [part[:, c * LINE : (c + 1) * LINE].astype(F32) for c in range(LINES)]
    starts = starts_ref[...].astype(F32)
    for k in range(3):
        rows += [jnp.broadcast_to(starts[k : k + 1, line : line + 1], (1, CH)) for line in range(LINES)]
    rows.append(jnp.zeros((EXTRA - len(rows), CH), F32))
    extra_ref[...] = jnp.concatenate(rows, axis=0).astype(BF16)
    for copy in copies[2:]:
        copy.wait()


def read_tables(pieces, order_ref, starts_ref):
    zone, _ = place_of()
    for back, ref in enumerate(pieces):
        m = wrap(zone - back + CHIPS)
        extra = ref[CELLS : CELLS + EXTRA, :].astype(F32)
        for k in range(3):
            for c in range(LINES):
                high = extra[8 * k + c : 8 * k + c + 1]
                low = extra[8 * k + 4 + c : 8 * k + 5 + c]
                order_ref[k, m, :, c * LINE : (c + 1) * LINE] = (2.0 * high + low).astype(I32)
            starts_ref[k, m] = extra[24 + 4 * k : 28 + 4 * k]


def gathered_rows(pieces, m, k):
    zone, core = place_of()
    rows = []
    for odd in range(2):
        for back, ref in enumerate(pieces):
            home = 2 * (zone - back) + jnp.bitwise_xor(core, odd)
            block = wrap(m - (k // 2) * home + NL)
            rows.append(ref[pl.ds(pl.multiple_of(odd * HALF + block * Q, Q), Q), :])
    return jnp.concatenate(rows, axis=0)


def moved_rows(same_ref, swap_ref, m):
    return jnp.concatenate([same_ref[m].reshape(HALF, CH), swap_ref[m].reshape(HALF, CH)], axis=0)


def forward_kernel(k, *refs):
    if k == 0:
        pieces, refs = refs[:CHIPS], refs[CHIPS:]
        gain_ref, taps_ref, mix_ref, order_ref, starts_ref, same_ref, swap_ref, x_ref, h_ref, pad = refs
        read_tables(pieces, order_ref, starts_ref)
    else:
        (in_ref, in_swap_ref, gain_ref, taps_ref, mix_ref, order_ref, starts_ref) = refs[:7]
        same_ref, swap_ref, x_ref, h_ref, pad = refs[7:]
    clear(pad)

    def holder(m, carry):
        received = gathered_rows(pieces, m, k) if k == 0 else moved_rows(in_ref, in_swap_ref, m)
        order = order_ref[k, m]
        row = block_row(order, k == 0)
        after = []
        for line in range(LINES):
            x = dot(picks(row, line), received, 1, 0)
            state, new = forward_line(
                k, x, starts_ref[k, m, line : line + 1, :], gain_ref, taps_ref, mix_ref, pad.at[line]
            )
            x_ref[m, line] = x.astype(BF16)
            h_ref[m, line] = state[4]
            after.append(new)
        put_next(block_row(order, False), jnp.concatenate(after, axis=0), m, 1, same_ref, swap_ref)
        return carry

    lax.fori_loop(0, CHIPS, holder, 0)


def turn_kernel(*refs):
    k = 2
    in_ref, in_swap_ref = refs[:2]
    pieces = refs[2 : 2 + CHIPS]
    gain_ref, taps_ref, mix_ref, order_ref, starts_ref = refs[2 + CHIPS : 7 + CHIPS]
    same_ref, swap_ref, own_ref, home_ref, sum_ref, pad, rows_ref = refs[7 + CHIPS :]
    clear(pad)
    start_sums(sum_ref, rows_ref)

    def holder(m, carry):
        received = moved_rows(in_ref, in_swap_ref, m)
        cot = gathered_rows(pieces, m, k)
        order = order_ref[k, m]
        row = block_row(order, False)
        cot_row = block_row(order, True)
        sums = new_sums()
        after, grads = [], []
        for line in range(LINES):
            x = dot(picks(row, line), received, 1, 0)
            state, new = forward_line(
                k, x, starts_ref[k, m, line : line + 1, :], gain_ref, taps_ref, mix_ref, pad.at[line]
            )
            after.append(new)
            grad = dot(picks(cot_row, line), cot, 1, 0).astype(BF16)
            grads.append(backward_line(k, grad, state, gain_ref, taps_ref, mix_ref, pad.at[line], sums))
        put_home(row, jnp.concatenate(after, axis=0), m, own_ref, home_ref)
        put_next(row, jnp.concatenate(grads, axis=0), m, -1, same_ref, swap_ref)
        add_sums(sum_ref, rows_ref, sums)
        return carry

    lax.fori_loop(0, CHIPS, holder, 0)
    end_sums(sum_ref, rows_ref)


def ring_of():
    return jnp.bitwise_and(lax.axis_index("dp"), RING - 1)


def share_out(sum_refs, small_ref, keep_ref, send_ref):
    _, core = place_of()
    here = ring_of()
    for r in range(NL):
        for k, ref in enumerate(sum_refs):
            small_ref[r, 2 * k : 2 * k + 2, :] = ref[CH + 2 * r : CH + 2 * r + 2, :]
        small_ref[r, 6:8, :] = jnp.zeros((2, CH), F32)
    for side, out in ((core, keep_ref), (1 - core, send_ref)):
        for ahead in range(RING):
            r = 2 * jnp.bitwise_and(here + ahead, RING - 1) + side
            for k, ref in enumerate(sum_refs):
                out[ahead, k * 16 : (k + 1) * 16, :] = ref[pl.ds(pl.multiple_of(r * 16, 16), 16), :]
            out[ahead, 48:SHARE, :] = small_ref[r]


def backward_kernel(k, *refs):
    in_ref, in_swap_ref, x_ref, h_ref, gain_ref, taps_ref, mix_ref, order_ref, starts_ref = refs[:9]
    if k == 1:
        same_ref, swap_ref, sum_ref, pad, rows_ref = refs[9:]
    else:
        sum1_ref, sum2_ref, first_ref, second_ref = refs[9:13]
        imitated_ref, own_ref, home_ref, keep_ref, send_ref, pad, rows_ref, sum_ref, small_ref = refs[13:]
        zone, core = place_of()
        for m in range(CHIPS):
            for ref, first in ((first_ref, 2 * m - core), (second_ref, 2 * m + 1 - 3 * core)):
                b = jnp.bitwise_and(first - 4 * zone + 4 * NL, NL - 1)
                imitated_ref[0, pl.ds(pl.multiple_of(b * Q, Q), Q), :] = ref[m]
    clear(pad)
    start_sums(sum_ref, rows_ref)

    def holder(m, carry):
        received = moved_rows(in_ref, in_swap_ref, m)
        row = block_row(order_ref[k, m], False)
        sums = new_sums()
        grads = []
        for line in range(LINES):
            grad = dot(picks(row, line), received, 1, 0).astype(BF16)
            hidden = h_ref[m, line]
            inverse, scaled, masked, keep = norm(
                x_ref[m, line].astype(F32), gain_ref[k : k + 1, :], starts_ref[k, m, line : line + 1, :]
            )
            gate = sigmoid(hidden)
            state = (inverse, scaled, masked, keep, hidden, gate, (hidden * gate).astype(BF16))
            grads.append(backward_line(k, grad, state, gain_ref, taps_ref, mix_ref, pad.at[line], sums))
        if k == 1:
            put_next(row, jnp.concatenate(grads, axis=0), m, -1, same_ref, swap_ref)
        else:
            put_home(row, jnp.concatenate(grads, axis=0), m, own_ref, home_ref)
        add_sums(sum_ref, rows_ref, sums)
        return carry

    lax.fori_loop(0, CHIPS, holder, 0)
    end_sums(sum_ref, rows_ref)
    if k == 0:
        share_out((sum_ref, sum1_ref, sum2_ref), small_ref, keep_ref, send_ref)


def finish_kernel(own_ref, other_ref, grad_ref, home_ref, mix_ref, taps_ref, gain_ref, out_ref, tail_ref):
    _, core = place_of()
    here = ring_of()
    for m in range(CHIPS):
        for ref, b in ((grad_ref, 2 * m + core), (home_ref, 2 * m + 1 - core)):
            out_ref[0, pl.ds(pl.multiple_of(b * Q, Q), Q), :] = ref[m]
    for ref, side in ((own_ref, core), (other_ref, 1 - core)):
        for back in range(RING):
            r = 2 * jnp.bitwise_and(here - back + RING, RING - 1) + side
            for k in range(3):
                mix_ref[k, pl.ds(pl.multiple_of(r * 16, 16), 16), :] = ref[back, k * 16 : (k + 1) * 16, :]
            tail_ref[r] = ref[back, 48:SHARE, :]
    for k in range(3):
        for r in range(NL):
            pair = tail_ref[r, 2 * k : 2 * k + 2, :]
            if r < NL - 1:
                taps_ref[k, 2 * r : 2 * r + 2, :] = pair
            else:
                taps_ref[k, 2 * r : 2 * r + 1, :] = pair[0:1]
                gain_ref[k : k + 1, :] = pair[1:2]


def call(kernel, outs, n_in, scratch=(), space=pltpu.VMEM, grant=VMEM_GRANT):
    vmem = pl.BlockSpec(memory_space=pltpu.VMEM)
    return pl.pallas_call(
        kernel,
        out_shape=outs,
        in_specs=[pl.BlockSpec(memory_space=space)] * n_in,
        out_specs=[vmem] * len(outs),
        scratch_shapes=[pltpu.VMEM(dims, F32) if isinstance(dims, tuple) else dims for dims in scratch],
        compiler_params=pltpu.CompilerParams(vmem_limit_bytes=grant),
    )


def shape(*dims, dtype=BF16):
    return jax.ShapeDtypeStruct(dims, dtype)


def swap(values):
    return lax.ppermute(values, "line", [(i, i ^ 1) for i in range(NL)])


def from_chips(values):
    got = {
        back: lax.ppermute(values, "line", [(i, (i + 2 * back) % NL) for i in range(NL)])
        for back in (2, 1, 3)
    }
    return [values, got[1], got[2], got[3]]


def to_ring(values, turn, ring, stride):
    pairs = []
    for i in range(lax.axis_size("dp")):
        at = i // stride % ring
        pairs.append((i, i + ((at + turn) % ring - at) * stride))
    return lax.ppermute(values, "dp", pairs)


def sum_over_dp(parts):
    size = lax.axis_size("dp")
    part = sum((to_ring(parts[turn], turn, RING, 1) for turn in (1, 3, 2)), parts[0])
    stride = RING
    while stride < size:
        ring = RING if size % (stride * RING) == 0 else 2
        part = sum((to_ring(part, turn, ring, stride) for turn in range(1, ring)), part)
        stride *= ring
    return part


def block(fields, cotangent, norm_gain, kernel, mix_weight, line_order, line_starts):
    dp_size = lax.axis_size("dp")
    weights = (norm_gain, kernel, mix_weight)
    quarter = shape(CHIPS, Q, CH)
    moving = shape(CHIPS, CHIPS, Q, CH)
    tables = (shape(3, CHIPS, 1, CELLS, dtype=I32), shape(3, CHIPS, LINES, CH, dtype=F32))
    state = (shape(CHIPS, LINES, LINE, CH), shape(CHIPS, LINES, LINE, CH, dtype=F32))
    sums = shape(ROWS, CH, dtype=F32)
    pad = (LINES, LINE + 16, CH)
    parts = (TAPS + 1, 8, CH)

    keep, keep_cot, send, extra = call(
        prep_kernel,
        (quarter, quarter, shape(NL, Q, CH), shape(EXTRA, CH)),
        4,
        scratch=(pltpu.VMEM((3, CELLS), I32), pltpu.VMEM((3, LINES), I32), pltpu.SemaphoreType.DMA((18,))),
        space=pltpu.HBM,
        grant=None,
    )(fields, cotangent, line_order, line_starts)
    got = swap(send)
    piece = jnp.concatenate([keep.reshape(HALF, CH), got[:CHIPS].reshape(HALF, CH), extra])
    piece_cot = jnp.concatenate([keep_cot.reshape(HALF, CH), got[CHIPS:].reshape(HALF, CH)])
    pieces = from_chips(piece)
    pieces_cot = from_chips(piece_cot)
    order, starts, same, moved, x0, h0 = call(
        functools.partial(forward_kernel, 0), (*tables, moving, moving, *state), 7, scratch=(pad,)
    )(*pieces, *weights)
    given = (*weights, order, starts)
    same, moved, x1, h1 = call(
        functools.partial(forward_kernel, 1), (moving, moving, *state), 7, scratch=(pad,)
    )(same, swap(moved), *given)
    same, moved, first, second, sums2 = call(
        turn_kernel, (moving, moving, quarter, quarter, sums), 11, scratch=(pad, parts)
    )(same, swap(moved), *pieces_cot, *given)
    second = swap(second)
    moved = swap(moved)
    same, moved, sums1 = call(
        functools.partial(backward_kernel, 1), (moving, moving, sums), 9, scratch=(pad, parts)
    )(same, moved, x1, h1, *given)
    share = shape(RING, SHARE, CH, dtype=F32)
    imitated, own, home, keep, send = call(
        functools.partial(backward_kernel, 0),
        (shape(1, CELLS, CH), quarter, quarter, share, share),
        13,
        scratch=(pad, parts, (ROWS, CH), (NL, 8, CH)),
    )(same, swap(moved), x0, h0, *given, sums1, sums2, first, second)
    grad_scale = float(dp_size * NL * CELLS) ** (-0.5)
    got = swap(send)
    home = swap(home)
    part = sum_over_dp(keep + got) * grad_scale
    shares = jnp.stack([part] + [to_ring(part, turn, RING, 1) for turn in range(1, RING)])
    mix_grad, kernel_grad, gain_grad, field_grad = call(
        finish_kernel,
        (
            shape(3, CH, CH, dtype=F32),
            shape(3, TAPS, CH, dtype=F32),
            shape(3, CH, dtype=F32),
            shape(1, CELLS, CH),
        ),
        4,
        scratch=((NL, 8, CH),),
    )(shares, swap(shares), own, home)
    return imitated, field_grad, mix_grad, kernel_grad, gain_grad


def solution(mesh):
    in_specs = (
        P("dp", "line", None),
        P("dp", "line", None),
        P(),
        P(),
        P(),
        P(None, "line"),
        P(None, "line"),
    )
    out_specs = (P("dp", "line", None), P("dp", "line", None), P(), P(), P())
    return jax.shard_map(block, mesh=mesh, in_specs=in_specs, out_specs=out_specs, check_vma=False)
```

```python
import functools

import jax
import jax.numpy as jnp
from jax import lax
from jax.experimental import pallas as pl
from jax.experimental.pallas import tpu as pltpu
from jax.sharding import PartitionSpec as P


LINE = 128
CH = 128
TAPS = 15
CELLS = 512
NL = 8
CHIPS = NL // 2
RING = 4
GROUP = 2
Q = CELLS // NL
HALF = CELLS // 2
LINES = CELLS // LINE
EPSILON = 1e-06
OFFSETS = [0] + [s * 2**level for level in range(7) for s in (-1, 1)]
F32 = jnp.float32
BF16 = jnp.bfloat16
I32 = jnp.int32
ROWS = LINE + TAPS + 1
EXTRA = 48
SHARE = 56
VMEM_GRANT = 12 * 2**20


def dot(a, b, ca, cb):
    return lax.dot_general(a, b, (((ca,), (cb,)), ((), ())), preferred_element_type=F32)


def place_of():
    me = lax.axis_index("line")
    return lax.shift_right_logical(me, 1), jnp.bitwise_and(me, 1)


def wrap(index):
    return jnp.bitwise_and(index, CHIPS - 1)


def block_row(order, gathered):
    home = lax.shift_right_logical(order, 6)
    within = jnp.bitwise_and(order, Q - 1)
    odd = jnp.bitwise_and(home, 1)
    chip = lax.shift_right_logical(home, 1)
    if gathered:
        zone, core = place_of()
        odd = jnp.bitwise_xor(odd, core)
        chip = wrap(zone - chip + CHIPS)
    return odd * HALF + chip * Q + within


def picks(row, line):
    part = row[:, line * LINE : (line + 1) * LINE]
    wanted = jnp.transpose(jnp.broadcast_to(part, (LINE, LINE)))
    lanes = lax.broadcasted_iota(I32, (LINE, LINE), 1)
    return jnp.concatenate(
        [jnp.where(wanted == lanes + c * LINE, 1.0, 0.0).astype(BF16) for c in range(LINES)],
        axis=1,
    )


def place(row, values, rows):
    hot = jnp.where(jnp.broadcast_to(row, (LINE, CELLS)) == rows, 1.0, 0.0).astype(BF16)
    return dot(hot, values, 1, 0).astype(BF16)


def put_next(row, values, m, sign, same_ref, swap_ref):
    _, core = place_of()
    for c in range(LINES):
        rows = lax.broadcasted_iota(I32, (LINE, CELLS), 0) + c * LINE
        placed = place(row, values, rows)
        for half in range(2):
            h = (c * 2 + half) % CHIPS
            block = placed[half * Q : (half + 1) * Q]
            if c < LINES // 2:
                same_ref[wrap(m + sign * h + CHIPS), h] = block
            else:
                at = m + h + core if sign > 0 else m - h - 1 + core + CHIPS
                swap_ref[wrap(at), h] = block


def put_home(row, values, m, own_ref, swap_ref):
    zone, core = place_of()
    step = lax.broadcasted_iota(I32, (LINE, CELLS), 0)
    mine = (core * CHIPS + zone) * Q
    other = ((1 - core) * CHIPS + zone) * Q - Q
    placed = place(row, values, step + jnp.where(step < Q, mine, other))
    own_ref[m] = placed[:Q]
    swap_ref[m] = placed[Q:]


def shifts(pad, values):
    pad[8 : 8 + LINE, :] = values
    for offset in OFFSETS:
        if offset == 0:
            yield 0, values
        elif abs(offset) < 8:
            yield 0, pad[8 + offset : 8 + offset + LINE, :]
        elif offset > 0:
            yield 0, values[offset:]
        else:
            yield -offset, values[:offset]


def accumulate(total, first, rows):
    size = rows.shape[0]
    pieces = [total[:first]] if first else []
    pieces.append(total[first : first + size] + rows)
    if first + size < LINE:
        pieces.append(total[first + size :])
    return jnp.concatenate(pieces, axis=0) if len(pieces) > 1 else pieces[0]


def clear(pads):
    edge = jnp.zeros((GROUP, LINES, 8, CH), F32)
    pads[:, :, 0:8, :] = edge
    pads[:, :, 8 + LINE : 16 + LINE, :] = edge


def norm(x, gain, start):
    inverse = lax.rsqrt(jnp.mean(x * x, axis=-1, keepdims=True) + EPSILON)
    scaled = x * inverse
    normed = (scaled * gain).astype(BF16).astype(F32)
    keep = lax.broadcasted_iota(I32, (LINE, CH), 0).astype(F32) >= start
    return inverse, scaled, jnp.where(keep, normed, 0.0), keep


def conv(pad, masked, taps):
    total = None
    for t, (first, moved) in enumerate(shifts(pad, masked)):
        term = taps[t : t + 1, :] * moved
        total = term if total is None else accumulate(total, first, term)
    return total


def sigmoid(h):
    return 1.0 / (1.0 + jnp.exp(-h))


def gather_stage(row, received, out):
    for line in range(LINES):
        out[line] = dot(picks(row, line), received, 1, 0).astype(BF16)


def hidden_stage(k, x_at, start_at, h_at, active, gain_ref, taps_ref, pads, line):
    x = x_at[line].astype(F32)
    masked = norm(x, gain_ref[k : k + 1, :], start_at[line : line + 1, :])[2]
    hidden = conv(pads.at[line], masked, taps_ref[k])
    h_at[line] = hidden
    active[line] = (hidden * sigmoid(hidden)).astype(BF16)


def mix_stage(k, x_at, active, mix_ref):
    mixed = dot(active[...].reshape(CELLS, CH), mix_ref[k], 1, 0).astype(BF16).astype(F32)
    return (x_at[...].reshape(CELLS, CH).astype(F32) + mixed).astype(BF16)


def activity_stage(h_at, active):
    for line in range(LINES):
        hidden = h_at[line]
        active[line] = (hidden * sigmoid(hidden)).astype(BF16)


def slope_stage(k, grad_at, h_at, slope_at, mix_ref):
    grad_act = dot(grad_at[...].reshape(CELLS, CH), mix_ref[k], 1, 1).reshape(LINES, LINE, CH)
    for line in range(LINES):
        hidden = h_at[line]
        gate = sigmoid(hidden)
        slope_at[line] = (grad_act[line] * (gate * (1.0 + hidden * (1.0 - gate)))).astype(BF16)


def backward_line(k, grad_at, x_at, start_at, slope_at, gain_ref, taps_ref, pads, line, sums):
    gain = gain_ref[k : k + 1, :]
    taps = taps_ref[k]
    inverse, scaled, masked, keep = norm(x_at[line].astype(F32), gain, start_at[line : line + 1, :])
    total = None
    for t, (first, moved) in enumerate(shifts(pads.at[line], slope_at[line].astype(F32))):
        u = t if t == 0 else (t + 1 if t % 2 else t - 1)
        size = moved.shape[0]
        term = taps[u : u + 1, :] * moved
        total = term if total is None else accumulate(total, first, term)
        part = jnp.sum((moved * masked[first : first + size]).reshape(size // 8, 8, CH), axis=0)
        sums[u] = part if sums[u] is None else sums[u] + part
    cells = jnp.where(keep, total, 0.0).astype(BF16).astype(F32)
    part = jnp.sum((cells * scaled).reshape(LINE // 8, 8, CH), axis=0)
    sums[TAPS] = part if sums[TAPS] is None else sums[TAPS] + part
    weighted = cells * gain
    moved = inverse * (weighted - scaled * jnp.mean(weighted * scaled, axis=-1, keepdims=True))
    return (grad_at[line].astype(F32) + moved).astype(BF16)


def add_sums(sum_ref, rows_ref, active, grad_at, sums):
    sum_ref[0:CH, :] += dot(active[...].reshape(CELLS, CH), grad_at[...].reshape(CELLS, CH), 0, 0)
    for t, part in enumerate(sums):
        rows_ref[t] += part


def start_sums(sum_ref, rows_ref):
    sum_ref[...] = jnp.zeros_like(sum_ref)
    rows_ref[...] = jnp.zeros_like(rows_ref)


def end_sums(sum_ref, rows_ref):
    sum_ref[CH:ROWS, :] = jnp.sum(rows_ref[...], axis=1)


def prep_kernel(fields_ref, cot_ref, table_ref, begin_ref, keep_ref, keep_cot_ref, send_ref, extra_ref, order_ref, starts_ref, sem):
    _, core = place_of()
    copies = [
        pltpu.make_async_copy(table_ref, order_ref, sem.at[0]),
        pltpu.make_async_copy(begin_ref, starts_ref, sem.at[1]),
    ]
    for m in range(CHIPS):
        here = pl.ds(pl.multiple_of((2 * m + core) * Q, Q), Q)
        there = pl.ds(pl.multiple_of((2 * m + 1 - core) * Q, Q), Q)
        for source, own, first in ((fields_ref, keep_ref, 0), (cot_ref, keep_cot_ref, CHIPS)):
            for rows, target in ((here, own.at[m]), (there, send_ref.at[first + m])):
                copies.append(pltpu.make_async_copy(source.at[0, rows, :], target, sem.at[len(copies)]))
    for copy in copies:
        copy.start()
    for copy in copies[:2]:
        copy.wait()
    rows = []
    for k in range(3):
        order = order_ref[k : k + 1, :]
        for part in (lax.shift_right_logical(order, 1), jnp.bitwise_and(order, 1)):
            rows += [part[:, c * LINE : (c + 1) * LINE].astype(F32) for c in range(LINES)]
    starts = starts_ref[...].astype(F32)
    for k in range(3):
        rows += [jnp.broadcast_to(starts[k : k + 1, line : line + 1], (1, CH)) for line in range(LINES)]
    rows.append(jnp.zeros((EXTRA - len(rows), CH), F32))
    extra_ref[...] = jnp.concatenate(rows, axis=0).astype(BF16)
    for copy in copies[2:]:
        copy.wait()


def read_tables(pieces, order_ref, starts_ref):
    zone, _ = place_of()
    for back, ref in enumerate(pieces):
        m = wrap(zone - back + CHIPS)
        extra = ref[CELLS : CELLS + EXTRA, :].astype(F32)
        for k in range(3):
            for c in range(LINES):
                high = extra[8 * k + c : 8 * k + c + 1]
                low = extra[8 * k + 4 + c : 8 * k + 5 + c]
                order_ref[k, m, :, c * LINE : (c + 1) * LINE] = (2.0 * high + low).astype(I32)
            starts_ref[k, m] = extra[24 + 4 * k : 28 + 4 * k]


def gathered_rows(pieces, m, k):
    zone, core = place_of()
    rows = []
    for odd in range(2):
        for back, ref in enumerate(pieces):
            home = 2 * (zone - back) + jnp.bitwise_xor(core, odd)
            block = wrap(m - (k // 2) * home + NL)
            rows.append(ref[pl.ds(pl.multiple_of(odd * HALF + block * Q, Q), Q), :])
    return jnp.concatenate(rows, axis=0)


def moved_rows(same_ref, swap_ref, m):
    return jnp.concatenate([same_ref[m].reshape(HALF, CH), swap_ref[m].reshape(HALF, CH)], axis=0)


def forward_kernel(k, *refs):
    if k == 0:
        pieces, refs = refs[:CHIPS], refs[CHIPS:]
        gain_ref, taps_ref, mix_ref, order_ref, starts_ref, same_ref, swap_ref, x_ref, h_ref, pad, active = refs
        read_tables(pieces, order_ref, starts_ref)
    else:
        (in_ref, in_swap_ref, gain_ref, taps_ref, mix_ref, order_ref, starts_ref) = refs[:7]
        same_ref, swap_ref, x_ref, h_ref, pad, active = refs[7:]
    clear(pad)

    def holders(i, carry):
        ms = [i * GROUP + g for g in range(GROUP)]
        rows = []
        for m in ms:
            received = gathered_rows(pieces, m, k) if k == 0 else moved_rows(in_ref, in_swap_ref, m)
            rows.append(order_ref[k, m])
            gather_stage(block_row(rows[-1], k == 0), received, x_ref.at[m])
        for g, m in enumerate(ms):
            for line in range(LINES):
                hidden_stage(
                    k, x_ref.at[m], starts_ref.at[k, m], h_ref.at[m], active.at[g], gain_ref, taps_ref, pad.at[g], line
                )
        after = [mix_stage(k, x_ref.at[m], active.at[g], mix_ref) for g, m in enumerate(ms)]
        for g, m in enumerate(ms):
            put_next(block_row(rows[g], False), after[g], m, 1, same_ref, swap_ref)
        return carry

    lax.fori_loop(0, CHIPS // GROUP, holders, 0)


def turn_kernel(*refs):
    k = 2
    in_ref, in_swap_ref = refs[:2]
    pieces = refs[2 : 2 + CHIPS]
    gain_ref, taps_ref, mix_ref, order_ref, starts_ref = refs[2 + CHIPS : 7 + CHIPS]
    same_ref, swap_ref, own_ref, home_ref, sum_ref = refs[7 + CHIPS : 12 + CHIPS]
    pad, rows_ref, active, x_ref, grad_ref, slope_ref, h_ref = refs[12 + CHIPS :]
    clear(pad)
    start_sums(sum_ref, rows_ref)

    def holders(i, carry):
        ms = [i * GROUP + g for g in range(GROUP)]
        rows = []
        for g, m in enumerate(ms):
            order = order_ref[k, m]
            rows.append(block_row(order, False))
            gather_stage(rows[-1], moved_rows(in_ref, in_swap_ref, m), x_ref.at[g])
            gather_stage(block_row(order, True), gathered_rows(pieces, m, k), grad_ref.at[g])
        for g, m in enumerate(ms):
            for line in range(LINES):
                hidden_stage(
                    k, x_ref.at[g], starts_ref.at[k, m], h_ref.at[g], active.at[g], gain_ref, taps_ref, pad.at[g], line
                )
        for g, m in enumerate(ms):
            after = mix_stage(k, x_ref.at[g], active.at[g], mix_ref)
            slope_stage(k, grad_ref.at[g], h_ref.at[g], slope_ref.at[g], mix_ref)
            put_home(rows[g], after, m, own_ref, home_ref)
        for g, m in enumerate(ms):
            sums = [None] * (TAPS + 1)
            grads = [
                backward_line(
                    k, grad_ref.at[g], x_ref.at[g], starts_ref.at[k, m], slope_ref.at[g], gain_ref, taps_ref, pad.at[g], line, sums
                )
                for line in range(LINES)
            ]
            add_sums(sum_ref, rows_ref, active.at[g], grad_ref.at[g], sums)
            put_next(rows[g], jnp.concatenate(grads, axis=0), m, -1, same_ref, swap_ref)
        return carry

    lax.fori_loop(0, CHIPS // GROUP, holders, 0)
    end_sums(sum_ref, rows_ref)


def ring_of():
    return jnp.bitwise_and(lax.axis_index("dp"), RING - 1)


def share_out(sum_refs, small_ref, keep_ref, send_ref):
    _, core = place_of()
    here = ring_of()
    for r in range(NL):
        for k, ref in enumerate(sum_refs):
            small_ref[r, 2 * k : 2 * k + 2, :] = ref[CH + 2 * r : CH + 2 * r + 2, :]
        small_ref[r, 6:8, :] = jnp.zeros((2, CH), F32)
    for side, out in ((core, keep_ref), (1 - core, send_ref)):
        for ahead in range(RING):
            r = 2 * jnp.bitwise_and(here + ahead, RING - 1) + side
            for k, ref in enumerate(sum_refs):
                out[ahead, k * 16 : (k + 1) * 16, :] = ref[pl.ds(pl.multiple_of(r * 16, 16), 16), :]
            out[ahead, 48:SHARE, :] = small_ref[r]


def backward_kernel(k, *refs):
    in_ref, in_swap_ref, x_ref, h_ref, gain_ref, taps_ref, mix_ref, order_ref, starts_ref = refs[:9]
    if k == 1:
        same_ref, swap_ref, sum_ref, pad, rows_ref, active, grad_ref, slope_ref = refs[9:]
    else:
        sum1_ref, sum2_ref, first_ref, second_ref = refs[9:13]
        imitated_ref, own_ref, home_ref, keep_ref, send_ref = refs[13:18]
        pad, rows_ref, active, grad_ref, slope_ref, sum_ref, small_ref = refs[18:]
        zone, core = place_of()
        for m in range(CHIPS):
            for ref, first in ((first_ref, 2 * m - core), (second_ref, 2 * m + 1 - 3 * core)):
                b = jnp.bitwise_and(first - 4 * zone + 4 * NL, NL - 1)
                imitated_ref[0, pl.ds(pl.multiple_of(b * Q, Q), Q), :] = ref[m]
    clear(pad)
    start_sums(sum_ref, rows_ref)

    def holders(i, carry):
        ms = [i * GROUP + g for g in range(GROUP)]
        rows = []
        for g, m in enumerate(ms):
            rows.append(block_row(order_ref[k, m], False))
            gather_stage(rows[-1], moved_rows(in_ref, in_swap_ref, m), grad_ref.at[g])
        for g, m in enumerate(ms):
            activity_stage(h_ref.at[m], active.at[g])
            slope_stage(k, grad_ref.at[g], h_ref.at[m], slope_ref.at[g], mix_ref)
        for g, m in enumerate(ms):
            sums = [None] * (TAPS + 1)
            grads = [
                backward_line(
                    k, grad_ref.at[g], x_ref.at[m], starts_ref.at[k, m], slope_ref.at[g], gain_ref, taps_ref, pad.at[g], line, sums
                )
                for line in range(LINES)
            ]
            add_sums(sum_ref, rows_ref, active.at[g], grad_ref.at[g], sums)
            values = jnp.concatenate(grads, axis=0)
            if k == 1:
                put_next(rows[g], values, m, -1, same_ref, swap_ref)
            else:
                put_home(rows[g], values, m, own_ref, home_ref)
        return carry

    lax.fori_loop(0, CHIPS // GROUP, holders, 0)
    end_sums(sum_ref, rows_ref)
    if k == 0:
        share_out((sum_ref, sum1_ref, sum2_ref), small_ref, keep_ref, send_ref)


def finish_kernel(own_ref, other_ref, grad_ref, home_ref, mix_ref, taps_ref, gain_ref, out_ref, tail_ref):
    _, core = place_of()
    here = ring_of()
    for m in range(CHIPS):
        for ref, b in ((grad_ref, 2 * m + core), (home_ref, 2 * m + 1 - core)):
            out_ref[0, pl.ds(pl.multiple_of(b * Q, Q), Q), :] = ref[m]
    for ref, side in ((own_ref, core), (other_ref, 1 - core)):
        for back in range(RING):
            r = 2 * jnp.bitwise_and(here - back + RING, RING - 1) + side
            for k in range(3):
                mix_ref[k, pl.ds(pl.multiple_of(r * 16, 16), 16), :] = ref[back, k * 16 : (k + 1) * 16, :]
            tail_ref[r] = ref[back, 48:SHARE, :]
    for k in range(3):
        for r in range(NL):
            pair = tail_ref[r, 2 * k : 2 * k + 2, :]
            if r < NL - 1:
                taps_ref[k, 2 * r : 2 * r + 2, :] = pair
            else:
                taps_ref[k, 2 * r : 2 * r + 1, :] = pair[0:1]
                gain_ref[k : k + 1, :] = pair[1:2]


def call(kernel, outs, n_in, scratch=(), space=pltpu.VMEM, grant=VMEM_GRANT):
    vmem = pl.BlockSpec(memory_space=pltpu.VMEM)
    return pl.pallas_call(
        kernel,
        out_shape=outs,
        in_specs=[pl.BlockSpec(memory_space=space)] * n_in,
        out_specs=[vmem] * len(outs),
        scratch_shapes=[pltpu.VMEM(dims, F32) if isinstance(dims, tuple) else dims for dims in scratch],
        compiler_params=pltpu.CompilerParams(vmem_limit_bytes=grant),
    )


def shape(*dims, dtype=BF16):
    return jax.ShapeDtypeStruct(dims, dtype)


def swap(values):
    return lax.ppermute(values, "line", [(i, i ^ 1) for i in range(NL)])


def from_chips(values):
    got = [values]
    for back in range(1, CHIPS):
        got.append(lax.ppermute(values, "line", [(i, (i + 2 * back) % NL) for i in range(NL)]))
    return got


def to_ring(values, turn, ring, stride):
    pairs = []
    for i in range(lax.axis_size("dp")):
        at = i // stride % ring
        pairs.append((i, i + ((at + turn) % ring - at) * stride))
    return lax.ppermute(values, "dp", pairs)


def sum_over_dp(parts):
    size = lax.axis_size("dp")
    part = sum((to_ring(parts[turn], turn, RING, 1) for turn in (1, 3, 2)), parts[0])
    stride = RING
    while stride < size:
        ring = RING if size % (stride * RING) == 0 else 2
        part = sum((to_ring(part, turn, ring, stride) for turn in range(1, ring)), part)
        stride *= ring
    return part


def block(fields, cotangent, norm_gain, kernel, mix_weight, line_order, line_starts):
    dp_size = lax.axis_size("dp")
    weights = (norm_gain, kernel, mix_weight)
    quarter = shape(CHIPS, Q, CH)
    moving = shape(CHIPS, CHIPS, Q, CH)
    tables = (shape(3, CHIPS, 1, CELLS, dtype=I32), shape(3, CHIPS, LINES, CH, dtype=F32))
    state = (shape(CHIPS, LINES, LINE, CH), shape(CHIPS, LINES, LINE, CH, dtype=F32))
    sums = shape(ROWS, CH, dtype=F32)
    pad = (GROUP, LINES, LINE + 16, CH)
    lines = pltpu.VMEM((GROUP, LINES, LINE, CH), BF16)
    parts = (TAPS + 1, 8, CH)
    back = (pad, parts, lines, lines, lines)

    keep, keep_cot, send, extra = call(
        prep_kernel,
        (quarter, quarter, shape(NL, Q, CH), shape(EXTRA, CH)),
        4,
        scratch=(pltpu.VMEM((3, CELLS), I32), pltpu.VMEM((3, LINES), I32), pltpu.SemaphoreType.DMA((18,))),
        space=pltpu.HBM,
        grant=None,
    )(fields, cotangent, line_order, line_starts)
    got = swap(send)
    piece = jnp.concatenate([keep.reshape(HALF, CH), got[:CHIPS].reshape(HALF, CH), extra])
    piece_cot = jnp.concatenate([keep_cot.reshape(HALF, CH), got[CHIPS:].reshape(HALF, CH)])
    pieces = from_chips(piece)
    pieces_cot = from_chips(piece_cot)
    order, starts, same, moved, x0, h0 = call(
        functools.partial(forward_kernel, 0), (*tables, moving, moving, *state), 7, scratch=(pad, lines)
    )(*pieces, *weights)
    given = (*weights, order, starts)
    same, moved, x1, h1 = call(
        functools.partial(forward_kernel, 1), (moving, moving, *state), 7, scratch=(pad, lines)
    )(same, swap(moved), *given)
    same, moved, first, second, sums2 = call(
        turn_kernel, (moving, moving, quarter, quarter, sums), 11, scratch=(pad, parts, lines, lines, lines, lines, (GROUP, LINES, LINE, CH))
    )(same, swap(moved), *pieces_cot, *given)
    second = swap(second)
    moved = swap(moved)
    same, moved, sums1 = call(
        functools.partial(backward_kernel, 1), (moving, moving, sums), 9, scratch=back
    )(same, moved, x1, h1, *given)
    share = shape(RING, SHARE, CH, dtype=F32)
    imitated, own, home, keep, send = call(
        functools.partial(backward_kernel, 0),
        (shape(1, CELLS, CH), quarter, quarter, share, share),
        13,
        scratch=(*back, (ROWS, CH), (NL, 8, CH)),
    )(same, swap(moved), x0, h0, *given, sums1, sums2, first, second)
    grad_scale = float(dp_size * NL * CELLS) ** (-0.5)
    got = swap(send)
    home = swap(home)
    part = sum_over_dp(keep + got) * grad_scale
    shares = jnp.stack([part] + [to_ring(part, turn, RING, 1) for turn in range(1, RING)])
    mix_grad, kernel_grad, gain_grad, field_grad = call(
        finish_kernel,
        (
            shape(3, CH, CH, dtype=F32),
            shape(3, TAPS, CH, dtype=F32),
            shape(3, CH, dtype=F32),
            shape(1, CELLS, CH),
        ),
        4,
        scratch=((NL, 8, CH),),
    )(shares, swap(shares), own, home)
    return imitated, field_grad, mix_grad, kernel_grad, gain_grad


def solution(mesh):
    in_specs = (
        P("dp", "line", None),
        P("dp", "line", None),
        P(),
        P(),
        P(),
        P(None, "line"),
        P(None, "line"),
    )
    out_specs = (P("dp", "line", None), P("dp", "line", None), P(), P(), P())
    return jax.shard_map(block, mesh=mesh, in_specs=in_specs, out_specs=out_specs, check_vma=False)
```

```python
import functools

import jax
import jax.numpy as jnp
from jax import lax
from jax.experimental import pallas as pl
from jax.experimental.pallas import tpu as pltpu
from jax.sharding import PartitionSpec as P


LINE = 128
CH = 128
TAPS = 15
CELLS = 512
NL = 8
CHIPS = NL // 2
RING = 4
GROUP = 2
Q = CELLS // NL
HALF = CELLS // 2
LINES = CELLS // LINE
EPSILON = 1e-06
OFFSETS = [0] + [s * 2**level for level in range(7) for s in (-1, 1)]
F32 = jnp.float32
BF16 = jnp.bfloat16
I32 = jnp.int32
ROWS = LINE + TAPS + 1
EXTRA = 48
SHARE = 56
VMEM_GRANT = 12 * 2**20


def dot(a, b, ca, cb):
    return lax.dot_general(a, b, (((ca,), (cb,)), ((), ())), preferred_element_type=F32)


def place_of():
    me = lax.axis_index("line")
    return lax.shift_right_logical(me, 1), jnp.bitwise_and(me, 1)


def wrap(index):
    return jnp.bitwise_and(index, CHIPS - 1)


def block_row(order, gathered):
    home = lax.shift_right_logical(order, 6)
    within = jnp.bitwise_and(order, Q - 1)
    odd = jnp.bitwise_and(home, 1)
    chip = lax.shift_right_logical(home, 1)
    if gathered:
        zone, core = place_of()
        odd = jnp.bitwise_xor(odd, core)
        chip = wrap(zone - chip + CHIPS)
    return odd * HALF + chip * Q + within


def picks(row, line):
    part = row[:, line * LINE : (line + 1) * LINE]
    wanted = jnp.transpose(jnp.broadcast_to(part, (LINE, LINE)))
    lanes = lax.broadcasted_iota(I32, (LINE, LINE), 1)
    return jnp.concatenate(
        [jnp.where(wanted == lanes + c * LINE, 1.0, 0.0).astype(BF16) for c in range(LINES)],
        axis=1,
    )


def place(row, values, rows):
    hot = jnp.where(jnp.broadcast_to(row, (LINE, CELLS)) == rows, 1.0, 0.0).astype(BF16)
    return dot(hot, values, 1, 0).astype(BF16)


def put_next(row, values, m, sign, same_ref, swap_ref):
    _, core = place_of()
    for c in range(LINES):
        rows = lax.broadcasted_iota(I32, (LINE, CELLS), 0) + c * LINE
        placed = place(row, values, rows)
        for half in range(2):
            h = (c * 2 + half) % CHIPS
            block = placed[half * Q : (half + 1) * Q]
            if c < LINES // 2:
                same_ref[wrap(m + sign * h + CHIPS), h] = block
            else:
                at = m + h + core if sign > 0 else m - h - 1 + core + CHIPS
                swap_ref[wrap(at), h] = block


def put_home(row, values, m, own_ref, swap_ref):
    zone, core = place_of()
    step = lax.broadcasted_iota(I32, (LINE, CELLS), 0)
    mine = (core * CHIPS + zone) * Q
    other = ((1 - core) * CHIPS + zone) * Q - Q
    placed = place(row, values, step + jnp.where(step < Q, mine, other))
    own_ref[m] = placed[:Q]
    swap_ref[m] = placed[Q:]


def shifts(pad, values):
    pad[8 : 8 + LINE, :] = values
    for offset in OFFSETS:
        if offset == 0:
            yield 0, values
        elif abs(offset) < 8:
            yield 0, pad[8 + offset : 8 + offset + LINE, :]
        elif offset > 0:
            yield 0, values[offset:]
        else:
            yield -offset, values[:offset]


def accumulate(total, first, rows):
    size = rows.shape[0]
    pieces = [total[:first]] if first else []
    pieces.append(total[first : first + size] + rows)
    if first + size < LINE:
        pieces.append(total[first + size :])
    return jnp.concatenate(pieces, axis=0) if len(pieces) > 1 else pieces[0]


def clear(pads):
    edge = jnp.zeros((GROUP, LINES, 8, CH), F32)
    pads[:, :, 0:8, :] = edge
    pads[:, :, 8 + LINE : 16 + LINE, :] = edge


def norm(x, gain, start):
    inverse = lax.rsqrt(jnp.mean(x * x, axis=-1, keepdims=True) + EPSILON)
    scaled = x * inverse
    normed = (scaled * gain).astype(BF16).astype(F32)
    return inverse, jnp.where(kept(start), normed, 0.0)


def kept(start):
    return lax.broadcasted_iota(I32, (LINE, CH), 0).astype(F32) >= start


def conv(pad, masked, taps):
    total = None
    for t, (first, moved) in enumerate(shifts(pad, masked)):
        term = taps[t : t + 1, :] * moved
        total = term if total is None else accumulate(total, first, term)
    return total


def sigmoid(h):
    return 1.0 / (1.0 + jnp.exp(-h))


def gather_stage(row, received, out):
    for line in range(LINES):
        out[line] = dot(picks(row, line), received, 1, 0).astype(BF16)


def hidden_stage(k, x_at, start_at, saved, gain_ref, taps_ref, pads, line):
    active, masked_at, inverse_at, slope_at = saved
    x = x_at[line].astype(F32)
    inverse, masked = norm(x, gain_ref[k : k + 1, :], start_at[line : line + 1, :])
    hidden = conv(pads.at[line], masked, taps_ref[k])
    gate = sigmoid(hidden)
    active[line] = (hidden * gate).astype(BF16)
    masked_at[line] = masked.astype(BF16)
    inverse_at[line] = jnp.broadcast_to(inverse, (LINE, CH))
    slope_at[line] = gate * (1.0 + hidden * (1.0 - gate))


def mix_stage(k, x_at, active, mix_ref):
    mixed = dot(active[...].reshape(CELLS, CH), mix_ref[k], 1, 0).astype(BF16).astype(F32)
    return (x_at[...].reshape(CELLS, CH).astype(F32) + mixed).astype(BF16)


def slope_stage(k, grad_at, slope_at, out, mix_ref):
    grad_act = dot(grad_at[...].reshape(CELLS, CH), mix_ref[k], 1, 1).reshape(LINES, LINE, CH)
    for line in range(LINES):
        out[line] = (grad_act[line] * slope_at[line]).astype(BF16)


def backward_line(k, grad_at, x_at, start_at, saved, hidden_at, gain_ref, taps_ref, pads, line, sums):
    gain = gain_ref[k : k + 1, :]
    taps = taps_ref[k]
    masked = saved[1][line].astype(F32)
    inverse = saved[2][line]
    scaled = x_at[line].astype(F32) * inverse
    keep = kept(start_at[line : line + 1, :])
    total = None
    for t, (first, moved) in enumerate(shifts(pads.at[line], hidden_at[line].astype(F32))):
        u = t if t == 0 else (t + 1 if t % 2 else t - 1)
        size = moved.shape[0]
        term = taps[u : u + 1, :] * moved
        total = term if total is None else accumulate(total, first, term)
        part = jnp.sum((moved * masked[first : first + size]).reshape(size // 8, 8, CH), axis=0)
        sums[u] = part if sums[u] is None else sums[u] + part
    cells = jnp.where(keep, total, 0.0).astype(BF16).astype(F32)
    part = jnp.sum((cells * scaled).reshape(LINE // 8, 8, CH), axis=0)
    sums[TAPS] = part if sums[TAPS] is None else sums[TAPS] + part
    weighted = cells * gain
    moved = inverse * (weighted - scaled * jnp.mean(weighted * scaled, axis=-1, keepdims=True))
    return (grad_at[line].astype(F32) + moved).astype(BF16)


def at(saved, index):
    return [ref.at[index] for ref in saved]


def add_sums(sum_ref, rows_ref, active, grad_at, sums):
    sum_ref[0:CH, :] += dot(active[...].reshape(CELLS, CH), grad_at[...].reshape(CELLS, CH), 0, 0)
    for t, part in enumerate(sums):
        rows_ref[t] += part


def start_sums(sum_ref, rows_ref):
    sum_ref[...] = jnp.zeros_like(sum_ref)
    rows_ref[...] = jnp.zeros_like(rows_ref)


def end_sums(sum_ref, rows_ref):
    sum_ref[CH:ROWS, :] = jnp.sum(rows_ref[...], axis=1)


def prep_kernel(fields_ref, cot_ref, table_ref, begin_ref, keep_ref, keep_cot_ref, send_ref, extra_ref, order_ref, starts_ref, sem):
    _, core = place_of()
    copies = [
        pltpu.make_async_copy(table_ref, order_ref, sem.at[0]),
        pltpu.make_async_copy(begin_ref, starts_ref, sem.at[1]),
    ]
    for m in range(CHIPS):
        here = pl.ds(pl.multiple_of((2 * m + core) * Q, Q), Q)
        there = pl.ds(pl.multiple_of((2 * m + 1 - core) * Q, Q), Q)
        for source, own, first in ((fields_ref, keep_ref, 0), (cot_ref, keep_cot_ref, CHIPS)):
            for rows, target in ((here, own.at[m]), (there, send_ref.at[first + m])):
                copies.append(pltpu.make_async_copy(source.at[0, rows, :], target, sem.at[len(copies)]))
    for copy in copies:
        copy.start()
    for copy in copies[:2]:
        copy.wait()
    rows = []
    for k in range(3):
        order = order_ref[k : k + 1, :]
        for part in (lax.shift_right_logical(order, 1), jnp.bitwise_and(order, 1)):
            rows += [part[:, c * LINE : (c + 1) * LINE].astype(F32) for c in range(LINES)]
    starts = starts_ref[...].astype(F32)
    for k in range(3):
        rows += [jnp.broadcast_to(starts[k : k + 1, line : line + 1], (1, CH)) for line in range(LINES)]
    rows.append(jnp.zeros((EXTRA - len(rows), CH), F32))
    extra_ref[...] = jnp.concatenate(rows, axis=0).astype(BF16)
    for copy in copies[2:]:
        copy.wait()


def read_tables(pieces, order_ref, starts_ref):
    zone, _ = place_of()
    for back, ref in enumerate(pieces):
        m = wrap(zone - back + CHIPS)
        extra = ref[CELLS : CELLS + EXTRA, :].astype(F32)
        for k in range(3):
            for c in range(LINES):
                high = extra[8 * k + c : 8 * k + c + 1]
                low = extra[8 * k + 4 + c : 8 * k + 5 + c]
                order_ref[k, m, :, c * LINE : (c + 1) * LINE] = (2.0 * high + low).astype(I32)
            starts_ref[k, m] = extra[24 + 4 * k : 28 + 4 * k]


def gathered_rows(pieces, m, k):
    zone, core = place_of()
    rows = []
    for odd in range(2):
        for back, ref in enumerate(pieces):
            home = 2 * (zone - back) + jnp.bitwise_xor(core, odd)
            block = wrap(m - (k // 2) * home + NL)
            rows.append(ref[pl.ds(pl.multiple_of(odd * HALF + block * Q, Q), Q), :])
    return jnp.concatenate(rows, axis=0)


def moved_rows(same_ref, swap_ref, m):
    return jnp.concatenate([same_ref[m].reshape(HALF, CH), swap_ref[m].reshape(HALF, CH)], axis=0)


def forward_kernel(k, *refs):
    if k == 0:
        pieces, refs = refs[:CHIPS], refs[CHIPS:]
        gain_ref, taps_ref, mix_ref, order_ref, starts_ref, same_ref, swap_ref, x_ref, *saved, pad = refs
        read_tables(pieces, order_ref, starts_ref)
    else:
        in_ref, in_swap_ref, gain_ref, taps_ref, mix_ref, order_ref, starts_ref = refs[:7]
        same_ref, swap_ref, x_ref, *saved, pad = refs[7:]
    clear(pad)

    def holders(i, carry):
        ms = [i * GROUP + g for g in range(GROUP)]
        rows = []
        for m in ms:
            received = gathered_rows(pieces, m, k) if k == 0 else moved_rows(in_ref, in_swap_ref, m)
            rows.append(order_ref[k, m])
            gather_stage(block_row(rows[-1], k == 0), received, x_ref.at[m])
        for g, m in enumerate(ms):
            for line in range(LINES):
                hidden_stage(
                    k, x_ref.at[m], starts_ref.at[k, m], at(saved, m), gain_ref, taps_ref, pad.at[g], line
                )
        after = [mix_stage(k, x_ref.at[m], saved[0].at[m], mix_ref) for m in ms]
        for g, m in enumerate(ms):
            put_next(block_row(rows[g], False), after[g], m, 1, same_ref, swap_ref)
        return carry

    lax.fori_loop(0, CHIPS // GROUP, holders, 0)


def turn_kernel(*refs):
    k = 2
    in_ref, in_swap_ref = refs[:2]
    pieces = refs[2 : 2 + CHIPS]
    gain_ref, taps_ref, mix_ref, order_ref, starts_ref = refs[2 + CHIPS : 7 + CHIPS]
    same_ref, swap_ref, own_ref, home_ref, sum_ref = refs[7 + CHIPS : 12 + CHIPS]
    pad, rows_ref, grad_ref, hidden_ref, x_ref, *saved = refs[12 + CHIPS :]
    clear(pad)
    start_sums(sum_ref, rows_ref)

    def holders(i, carry):
        ms = [i * GROUP + g for g in range(GROUP)]
        rows = []
        for g, m in enumerate(ms):
            order = order_ref[k, m]
            rows.append(block_row(order, False))
            gather_stage(rows[-1], moved_rows(in_ref, in_swap_ref, m), x_ref.at[g])
            gather_stage(block_row(order, True), gathered_rows(pieces, m, k), grad_ref.at[g])
        for g, m in enumerate(ms):
            for line in range(LINES):
                hidden_stage(
                    k, x_ref.at[g], starts_ref.at[k, m], at(saved, g), gain_ref, taps_ref, pad.at[g], line
                )
        for g, m in enumerate(ms):
            after = mix_stage(k, x_ref.at[g], saved[0].at[g], mix_ref)
            slope_stage(k, grad_ref.at[g], saved[3].at[g], hidden_ref.at[g], mix_ref)
            put_home(rows[g], after, m, own_ref, home_ref)
        for g, m in enumerate(ms):
            sums = [None] * (TAPS + 1)
            grads = [
                backward_line(
                    k,
                    grad_ref.at[g],
                    x_ref.at[g],
                    starts_ref.at[k, m],
                    at(saved, g),
                    hidden_ref.at[g],
                    gain_ref,
                    taps_ref,
                    pad.at[g],
                    line,
                    sums,
                )
                for line in range(LINES)
            ]
            add_sums(sum_ref, rows_ref, saved[0].at[g], grad_ref.at[g], sums)
            put_next(rows[g], jnp.concatenate(grads, axis=0), m, -1, same_ref, swap_ref)
        return carry

    lax.fori_loop(0, CHIPS // GROUP, holders, 0)
    end_sums(sum_ref, rows_ref)


def ring_of():
    return jnp.bitwise_and(lax.axis_index("dp"), RING - 1)


def share_out(sum_refs, small_ref, keep_ref, send_ref):
    _, core = place_of()
    here = ring_of()
    for r in range(NL):
        for k, ref in enumerate(sum_refs):
            small_ref[r, 2 * k : 2 * k + 2, :] = ref[CH + 2 * r : CH + 2 * r + 2, :]
        small_ref[r, 6:8, :] = jnp.zeros((2, CH), F32)
    for side, out in ((core, keep_ref), (1 - core, send_ref)):
        for ahead in range(RING):
            r = 2 * jnp.bitwise_and(here + ahead, RING - 1) + side
            for k, ref in enumerate(sum_refs):
                out[ahead, k * 16 : (k + 1) * 16, :] = ref[pl.ds(pl.multiple_of(r * 16, 16), 16), :]
            out[ahead, 48:SHARE, :] = small_ref[r]


def backward_kernel(k, *refs):
    in_ref, in_swap_ref, x_ref = refs[:3]
    saved = refs[3:7]
    gain_ref, taps_ref, mix_ref, order_ref, starts_ref = refs[7:12]
    if k == 1:
        same_ref, swap_ref, sum_ref, pad, rows_ref, grad_ref, hidden_ref = refs[12:]
    else:
        sum1_ref, sum2_ref, first_ref, second_ref = refs[12:16]
        imitated_ref, own_ref, home_ref, keep_ref, send_ref = refs[16:21]
        pad, rows_ref, grad_ref, hidden_ref, sum_ref, small_ref = refs[21:]
        zone, core = place_of()
        for m in range(CHIPS):
            for ref, first in ((first_ref, 2 * m - core), (second_ref, 2 * m + 1 - 3 * core)):
                b = jnp.bitwise_and(first - 4 * zone + 4 * NL, NL - 1)
                imitated_ref[0, pl.ds(pl.multiple_of(b * Q, Q), Q), :] = ref[m]
    clear(pad)
    start_sums(sum_ref, rows_ref)

    def holders(i, carry):
        ms = [i * GROUP + g for g in range(GROUP)]
        rows = []
        for g, m in enumerate(ms):
            rows.append(block_row(order_ref[k, m], False))
            gather_stage(rows[-1], moved_rows(in_ref, in_swap_ref, m), grad_ref.at[g])
        for g, m in enumerate(ms):
            slope_stage(k, grad_ref.at[g], saved[3].at[m], hidden_ref.at[g], mix_ref)
        for g, m in enumerate(ms):
            sums = [None] * (TAPS + 1)
            grads = [
                backward_line(
                    k,
                    grad_ref.at[g],
                    x_ref.at[m],
                    starts_ref.at[k, m],
                    at(saved, m),
                    hidden_ref.at[g],
                    gain_ref,
                    taps_ref,
                    pad.at[g],
                    line,
                    sums,
                )
                for line in range(LINES)
            ]
            add_sums(sum_ref, rows_ref, saved[0].at[m], grad_ref.at[g], sums)
            values = jnp.concatenate(grads, axis=0)
            if k == 1:
                put_next(rows[g], values, m, -1, same_ref, swap_ref)
            else:
                put_home(rows[g], values, m, own_ref, home_ref)
        return carry

    lax.fori_loop(0, CHIPS // GROUP, holders, 0)
    end_sums(sum_ref, rows_ref)
    if k == 0:
        share_out((sum_ref, sum1_ref, sum2_ref), small_ref, keep_ref, send_ref)


def finish_kernel(own_ref, other_ref, grad_ref, home_ref, mix_ref, taps_ref, gain_ref, out_ref, tail_ref):
    _, core = place_of()
    here = ring_of()
    for m in range(CHIPS):
        for ref, b in ((grad_ref, 2 * m + core), (home_ref, 2 * m + 1 - core)):
            out_ref[0, pl.ds(pl.multiple_of(b * Q, Q), Q), :] = ref[m]
    for ref, side in ((own_ref, core), (other_ref, 1 - core)):
        for back in range(RING):
            r = 2 * jnp.bitwise_and(here - back + RING, RING - 1) + side
            for k in range(3):
                mix_ref[k, pl.ds(pl.multiple_of(r * 16, 16), 16), :] = ref[back, k * 16 : (k + 1) * 16, :]
            tail_ref[r] = ref[back, 48:SHARE, :]
    for k in range(3):
        for r in range(NL):
            pair = tail_ref[r, 2 * k : 2 * k + 2, :]
            if r < NL - 1:
                taps_ref[k, 2 * r : 2 * r + 2, :] = pair
            else:
                taps_ref[k, 2 * r : 2 * r + 1, :] = pair[0:1]
                gain_ref[k : k + 1, :] = pair[1:2]


def call(kernel, outs, n_in, scratch=(), space=pltpu.VMEM, grant=VMEM_GRANT):
    vmem = pl.BlockSpec(memory_space=pltpu.VMEM)
    return pl.pallas_call(
        kernel,
        out_shape=outs,
        in_specs=[pl.BlockSpec(memory_space=space)] * n_in,
        out_specs=[vmem] * len(outs),
        scratch_shapes=[pltpu.VMEM(dims, F32) if isinstance(dims, tuple) else dims for dims in scratch],
        compiler_params=pltpu.CompilerParams(vmem_limit_bytes=grant),
    )


def shape(*dims, dtype=BF16):
    return jax.ShapeDtypeStruct(dims, dtype)


def swap(values):
    return lax.ppermute(values, "line", [(i, i ^ 1) for i in range(NL)])


def from_chips(values):
    got = [values]
    for back in range(1, CHIPS):
        got.append(lax.ppermute(values, "line", [(i, (i + 2 * back) % NL) for i in range(NL)]))
    return got


def to_ring(values, turn, ring, stride):
    pairs = []
    for i in range(lax.axis_size("dp")):
        at = i // stride % ring
        pairs.append((i, i + ((at + turn) % ring - at) * stride))
    return lax.ppermute(values, "dp", pairs)


def sum_over_dp(parts):
    size = lax.axis_size("dp")
    part = sum([to_ring(parts[turn], turn, RING, 1) for turn in range(1, RING)], parts[0])
    stride = RING
    while stride < size:
        ring = RING if size % (stride * RING) == 0 else 2
        part = sum([to_ring(part, turn, ring, stride) for turn in range(1, ring)], part)
        stride *= ring
    return part


def block(fields, cotangent, norm_gain, kernel, mix_weight, line_order, line_starts):
    dp_size = lax.axis_size("dp")
    weights = (norm_gain, kernel, mix_weight)
    quarter = shape(CHIPS, Q, CH)
    moving = shape(CHIPS, CHIPS, Q, CH)
    tables = (shape(3, CHIPS, 1, CELLS, dtype=I32), shape(3, CHIPS, LINES, CH, dtype=F32))
    kinds = (BF16, BF16, BF16, F32, F32)
    state = [shape(CHIPS, LINES, LINE, CH, dtype=kind) for kind in kinds]
    sums = shape(ROWS, CH, dtype=F32)
    pad = (GROUP, LINES, LINE + 16, CH)
    lines = pltpu.VMEM((GROUP, LINES, LINE, CH), BF16)
    parts = (TAPS + 1, 8, CH)
    back = (pad, parts, lines, lines)
    wide = (GROUP, LINES, LINE, CH)

    keep, keep_cot, send, extra = call(
        prep_kernel,
        (quarter, quarter, shape(NL, Q, CH), shape(EXTRA, CH)),
        4,
        scratch=(pltpu.VMEM((3, CELLS), I32), pltpu.VMEM((3, LINES), I32), pltpu.SemaphoreType.DMA((18,))),
        space=pltpu.HBM,
        grant=None,
    )(fields, cotangent, line_order, line_starts)
    got = swap(send)
    piece = jnp.concatenate([keep.reshape(HALF, CH), got[:CHIPS].reshape(HALF, CH), extra])
    piece_cot = jnp.concatenate([keep_cot.reshape(HALF, CH), got[CHIPS:].reshape(HALF, CH)])
    pieces = from_chips(piece)
    pieces_cot = from_chips(piece_cot)
    order, starts, same, moved, *saved0 = call(
        functools.partial(forward_kernel, 0), (*tables, moving, moving, *state), 7, scratch=(pad,)
    )(*pieces, *weights)
    given = (*weights, order, starts)
    same, moved, *saved1 = call(
        functools.partial(forward_kernel, 1), (moving, moving, *state), 7, scratch=(pad,)
    )(same, swap(moved), *given)
    same, moved, first, second, sums2 = call(
        turn_kernel, (moving, moving, quarter, quarter, sums), 11, scratch=(*back, lines, lines, lines, wide, wide)
    )(same, swap(moved), *pieces_cot, *given)
    second = swap(second)
    moved = swap(moved)
    same, moved, sums1 = call(
        functools.partial(backward_kernel, 1), (moving, moving, sums), 12, scratch=back
    )(same, moved, *saved1, *given)
    share = shape(RING, SHARE, CH, dtype=F32)
    imitated, own, home, keep, send = call(
        functools.partial(backward_kernel, 0),
        (shape(1, CELLS, CH), quarter, quarter, share, share),
        16,
        scratch=(*back, (ROWS, CH), (NL, 8, CH)),
    )(same, swap(moved), *saved0, *given, sums1, sums2, first, second)
    grad_scale = float(dp_size * NL * CELLS) ** (-0.5)
    got = swap(send)
    home = swap(home)
    part = sum_over_dp(keep + got) * grad_scale
    shares = jnp.stack([part] + [to_ring(part, turn, RING, 1) for turn in range(1, RING)])
    mix_grad, kernel_grad, gain_grad, field_grad = call(
        finish_kernel,
        (
            shape(3, CH, CH, dtype=F32),
            shape(3, TAPS, CH, dtype=F32),
            shape(3, CH, dtype=F32),
            shape(1, CELLS, CH),
        ),
        4,
        scratch=((NL, 8, CH),),
    )(shares, swap(shares), own, home)
    return imitated, field_grad, mix_grad, kernel_grad, gain_grad


def solution(mesh):
    in_specs = (
        P("dp", "line", None),
        P("dp", "line", None),
        P(),
        P(),
        P(),
        P(None, "line"),
        P(None, "line"),
    )
    out_specs = (P("dp", "line", None), P("dp", "line", None), P(), P(), P())
    return jax.shard_map(block, mesh=mesh, in_specs=in_specs, out_specs=out_specs, check_vma=False)
```

```python
import functools

import jax
import jax.numpy as jnp
from jax import lax
from jax.experimental import pallas as pl
from jax.experimental.pallas import tpu as pltpu
from jax.sharding import PartitionSpec as P


LINE = 128
CH = 128
TAPS = 15
CELLS = 512
NL = 8
CHIPS = NL // 2
RING = 4
GROUP = 2
Q = CELLS // NL
HALF = CELLS // 2
LINES = CELLS // LINE
EPSILON = 1e-06
OFFSETS = [0] + [s * 2**level for level in range(7) for s in (-1, 1)]
F32 = jnp.float32
BF16 = jnp.bfloat16
I32 = jnp.int32
ROWS = LINE + TAPS + 1
EXTRA = 48
SHARE = 56
VMEM_GRANT = 12 * 2**20


def dot(a, b, ca, cb):
    return lax.dot_general(a, b, (((ca,), (cb,)), ((), ())), preferred_element_type=F32)


def place_of():
    me = lax.axis_index("line")
    return lax.shift_right_logical(me, 1), jnp.bitwise_and(me, 1)


def wrap(index):
    return jnp.bitwise_and(index, CHIPS - 1)


def block_row(order, gathered):
    home = lax.shift_right_logical(order, 6)
    within = jnp.bitwise_and(order, Q - 1)
    odd = jnp.bitwise_and(home, 1)
    chip = lax.shift_right_logical(home, 1)
    if gathered:
        zone, core = place_of()
        odd = jnp.bitwise_xor(odd, core)
        chip = wrap(zone - chip + CHIPS)
    return odd * HALF + chip * Q + within


def picks(row, line):
    part = row[:, line * LINE : (line + 1) * LINE]
    wanted = jnp.transpose(jnp.broadcast_to(part, (LINE, LINE)))
    lanes = lax.broadcasted_iota(I32, (LINE, LINE), 1)
    return jnp.concatenate(
        [jnp.where(wanted == lanes + c * LINE, 1.0, 0.0).astype(BF16) for c in range(LINES)],
        axis=1,
    )


def place(row, values, rows):
    hot = jnp.where(jnp.broadcast_to(row, (LINE, CELLS)) == rows, 1.0, 0.0).astype(BF16)
    return dot(hot, values, 1, 0).astype(BF16)


def put_next(row, values, m, sign, same_ref, swap_ref):
    _, core = place_of()
    for c in range(LINES):
        rows = lax.broadcasted_iota(I32, (LINE, CELLS), 0) + c * LINE
        placed = place(row, values, rows)
        for half in range(2):
            h = (c * 2 + half) % CHIPS
            block = placed[half * Q : (half + 1) * Q]
            if c < LINES // 2:
                same_ref[wrap(m + sign * h + CHIPS), h] = block
            else:
                at = m + h + core if sign > 0 else m - h - 1 + core + CHIPS
                swap_ref[wrap(at), h] = block


def put_home(row, values, m, own_ref, swap_ref):
    zone, core = place_of()
    step = lax.broadcasted_iota(I32, (LINE, CELLS), 0)
    mine = (core * CHIPS + zone) * Q
    other = ((1 - core) * CHIPS + zone) * Q - Q
    placed = place(row, values, step + jnp.where(step < Q, mine, other))
    own_ref[m] = placed[:Q]
    swap_ref[m] = placed[Q:]


def shifts(pad, values):
    pad[8 : 8 + LINE, :] = values
    for offset in OFFSETS:
        if offset == 0:
            yield 0, values
        elif abs(offset) < 8:
            yield 0, pad[8 + offset : 8 + offset + LINE, :]
        elif offset > 0:
            yield 0, values[offset:]
        else:
            yield -offset, values[:offset]


def accumulate(total, first, rows):
    size = rows.shape[0]
    pieces = [total[:first]] if first else []
    pieces.append(total[first : first + size] + rows)
    if first + size < LINE:
        pieces.append(total[first + size :])
    return jnp.concatenate(pieces, axis=0) if len(pieces) > 1 else pieces[0]


def clear(pads):
    edge = jnp.zeros((GROUP, LINES, 8, CH), F32)
    pads[:, :, 0:8, :] = edge
    pads[:, :, 8 + LINE : 16 + LINE, :] = edge


def norm(x, gain, start):
    inverse = lax.rsqrt(jnp.mean(x * x, axis=-1, keepdims=True) + EPSILON)
    scaled = x * inverse
    normed = (scaled * gain).astype(BF16).astype(F32)
    return inverse, jnp.where(kept(start), normed, 0.0)


def kept(start):
    return lax.broadcasted_iota(I32, (LINE, CH), 0).astype(F32) >= start


def conv(pad, masked, taps):
    total = None
    for t, (first, moved) in enumerate(shifts(pad, masked)):
        term = taps[t : t + 1, :] * moved
        total = term if total is None else accumulate(total, first, term)
    return total


def sigmoid(h):
    return 1.0 / (1.0 + jnp.exp(-h))


def gather_stage(row, received, out):
    for line in range(LINES):
        out[line] = dot(picks(row, line), received, 1, 0).astype(BF16)


def hidden_stage(k, x_at, start_at, saved, gain_ref, taps_ref, pads, line):
    active, masked_at, inverse_at, slope_at = saved
    x = x_at[line].astype(F32)
    inverse, masked = norm(x, gain_ref[k : k + 1, :], start_at[line : line + 1, :])
    hidden = conv(pads.at[line], masked, taps_ref[k])
    gate = sigmoid(hidden)
    active[line] = (hidden * gate).astype(BF16)
    masked_at[line] = masked.astype(BF16)
    inverse_at[line] = jnp.broadcast_to(inverse, (LINE, CH))
    slope_at[line] = gate * (1.0 + hidden * (1.0 - gate))


def mix_stage(k, x_at, active, mix_ref):
    mixed = dot(active[...].reshape(CELLS, CH), mix_ref[k], 1, 0).astype(BF16).astype(F32)
    return (x_at[...].reshape(CELLS, CH).astype(F32) + mixed).astype(BF16)


def slope_stage(k, grad_at, slope_at, out, mix_ref):
    grad_act = dot(grad_at[...].reshape(CELLS, CH), mix_ref[k], 1, 1).reshape(LINES, LINE, CH)
    for line in range(LINES):
        out[line] = (grad_act[line] * slope_at[line]).astype(BF16)


def backward_line(k, grad_at, x_at, start_at, saved, hidden_at, gain_ref, taps_ref, pads, line, sums):
    gain = gain_ref[k : k + 1, :]
    taps = taps_ref[k]
    masked = saved[1][line].astype(F32)
    inverse = saved[2][line]
    scaled = x_at[line].astype(F32) * inverse
    keep = kept(start_at[line : line + 1, :])
    total = None
    for t, (first, moved) in enumerate(shifts(pads.at[line], hidden_at[line].astype(F32))):
        u = t if t == 0 else (t + 1 if t % 2 else t - 1)
        size = moved.shape[0]
        term = taps[u : u + 1, :] * moved
        total = term if total is None else accumulate(total, first, term)
        part = jnp.sum((moved * masked[first : first + size]).reshape(size // 8, 8, CH), axis=0)
        sums[u] = part if sums[u] is None else sums[u] + part
    cells = jnp.where(keep, total, 0.0).astype(BF16).astype(F32)
    part = jnp.sum((cells * scaled).reshape(LINE // 8, 8, CH), axis=0)
    sums[TAPS] = part if sums[TAPS] is None else sums[TAPS] + part
    weighted = cells * gain
    moved = inverse * (weighted - scaled * jnp.mean(weighted * scaled, axis=-1, keepdims=True))
    return (grad_at[line].astype(F32) + moved).astype(BF16)


def at(saved, index):
    return [ref.at[index] for ref in saved]


def add_sums(sum_ref, rows_ref, active, grad_at, sums):
    sum_ref[0:CH, :] += dot(active[...].reshape(CELLS, CH), grad_at[...].reshape(CELLS, CH), 0, 0)
    for t, part in enumerate(sums):
        rows_ref[t] += part


def start_sums(sum_ref, rows_ref):
    sum_ref[...] = jnp.zeros_like(sum_ref)
    rows_ref[...] = jnp.zeros_like(rows_ref)


def end_sums(sum_ref, rows_ref):
    sum_ref[CH:ROWS, :] = jnp.sum(rows_ref[...], axis=1)


def prep_kernel(fields_ref, cot_ref, table_ref, begin_ref, keep_ref, keep_cot_ref, send_ref, extra_ref, order_ref, starts_ref, sem):
    _, core = place_of()
    copies = [
        pltpu.make_async_copy(table_ref, order_ref, sem.at[0]),
        pltpu.make_async_copy(begin_ref, starts_ref, sem.at[1]),
    ]
    for m in range(CHIPS):
        here = pl.ds(pl.multiple_of((2 * m + core) * Q, Q), Q)
        there = pl.ds(pl.multiple_of((2 * m + 1 - core) * Q, Q), Q)
        for source, own, first in ((fields_ref, keep_ref, 0), (cot_ref, keep_cot_ref, CHIPS)):
            for rows, target in ((here, own.at[m]), (there, send_ref.at[first + m])):
                copies.append(pltpu.make_async_copy(source.at[0, rows, :], target, sem.at[len(copies)]))
    for copy in copies:
        copy.start()
    for copy in copies[:2]:
        copy.wait()
    rows = []
    for k in range(3):
        order = order_ref[k : k + 1, :]
        for part in (lax.shift_right_logical(order, 1), jnp.bitwise_and(order, 1)):
            rows += [part[:, c * LINE : (c + 1) * LINE].astype(F32) for c in range(LINES)]
    starts = starts_ref[...].astype(F32)
    for k in range(3):
        rows += [jnp.broadcast_to(starts[k : k + 1, line : line + 1], (1, CH)) for line in range(LINES)]
    rows.append(jnp.zeros((EXTRA - len(rows), CH), F32))
    extra_ref[...] = jnp.concatenate(rows, axis=0).astype(BF16)
    for copy in copies[2:]:
        copy.wait()


def read_tables(pieces, order_ref, starts_ref):
    zone, _ = place_of()
    for back, ref in enumerate(pieces):
        m = wrap(zone - back + CHIPS)
        extra = ref[CELLS : CELLS + EXTRA, :].astype(F32)
        for k in range(3):
            for c in range(LINES):
                high = extra[8 * k + c : 8 * k + c + 1]
                low = extra[8 * k + 4 + c : 8 * k + 5 + c]
                order_ref[k, m, :, c * LINE : (c + 1) * LINE] = (2.0 * high + low).astype(I32)
            starts_ref[k, m] = extra[24 + 4 * k : 28 + 4 * k]


def gathered_rows(pieces, m, k):
    zone, core = place_of()
    rows = []
    for odd in range(2):
        for back, ref in enumerate(pieces):
            home = 2 * (zone - back) + jnp.bitwise_xor(core, odd)
            block = wrap(m - (k // 2) * home + NL)
            rows.append(ref[pl.ds(pl.multiple_of(odd * HALF + block * Q, Q), Q), :])
    return jnp.concatenate(rows, axis=0)


def moved_rows(same_ref, swap_ref, m):
    return jnp.concatenate([same_ref[m].reshape(HALF, CH), swap_ref[m].reshape(HALF, CH)], axis=0)


def forward_kernel(k, *refs):
    if k == 0:
        pieces, refs = refs[:CHIPS], refs[CHIPS:]
        gain_ref, taps_ref, mix_ref, order_ref, starts_ref, same_ref, swap_ref, x_ref, *saved, pad = refs
        read_tables(pieces, order_ref, starts_ref)
    else:
        in_ref, in_swap_ref, gain_ref, taps_ref, mix_ref, order_ref, starts_ref = refs[:7]
        same_ref, swap_ref, x_ref, *saved, pad = refs[7:]
    clear(pad)

    def holders(i, carry):
        ms = [i * GROUP + g for g in range(GROUP)]
        rows = []
        for m in ms:
            received = gathered_rows(pieces, m, k) if k == 0 else moved_rows(in_ref, in_swap_ref, m)
            rows.append(order_ref[k, m])
            gather_stage(block_row(rows[-1], k == 0), received, x_ref.at[m])
        for g, m in enumerate(ms):
            for line in range(LINES):
                hidden_stage(
                    k, x_ref.at[m], starts_ref.at[k, m], at(saved, m), gain_ref, taps_ref, pad.at[g], line
                )
        after = [mix_stage(k, x_ref.at[m], saved[0].at[m], mix_ref) for m in ms]
        for g, m in enumerate(ms):
            put_next(block_row(rows[g], False), after[g], m, 1, same_ref, swap_ref)
        return carry

    lax.fori_loop(0, CHIPS // GROUP, holders, 0)


def turn_kernel(*refs):
    k = 2
    in_ref, in_swap_ref = refs[:2]
    pieces = refs[2 : 2 + CHIPS]
    gain_ref, taps_ref, mix_ref, order_ref, starts_ref = refs[2 + CHIPS : 7 + CHIPS]
    same_ref, swap_ref, own_ref, home_ref, sum_ref = refs[7 + CHIPS : 12 + CHIPS]
    pad, rows_ref, grad_ref, hidden_ref, x_ref, *saved = refs[12 + CHIPS :]
    clear(pad)
    start_sums(sum_ref, rows_ref)

    def holders(i, carry):
        ms = [i * GROUP + g for g in range(GROUP)]
        rows = []
        for g, m in enumerate(ms):
            order = order_ref[k, m]
            rows.append(block_row(order, False))
            gather_stage(rows[-1], moved_rows(in_ref, in_swap_ref, m), x_ref.at[g])
            gather_stage(block_row(order, True), gathered_rows(pieces, m, k), grad_ref.at[g])
        for g, m in enumerate(ms):
            for line in range(LINES):
                hidden_stage(
                    k, x_ref.at[g], starts_ref.at[k, m], at(saved, g), gain_ref, taps_ref, pad.at[g], line
                )
        for g, m in enumerate(ms):
            after = mix_stage(k, x_ref.at[g], saved[0].at[g], mix_ref)
            slope_stage(k, grad_ref.at[g], saved[3].at[g], hidden_ref.at[g], mix_ref)
            put_home(rows[g], after, m, own_ref, home_ref)
        for g, m in enumerate(ms):
            sums = [None] * (TAPS + 1)
            grads = [
                backward_line(
                    k,
                    grad_ref.at[g],
                    x_ref.at[g],
                    starts_ref.at[k, m],
                    at(saved, g),
                    hidden_ref.at[g],
                    gain_ref,
                    taps_ref,
                    pad.at[g],
                    line,
                    sums,
                )
                for line in range(LINES)
            ]
            add_sums(sum_ref, rows_ref, saved[0].at[g], grad_ref.at[g], sums)
            put_next(rows[g], jnp.concatenate(grads, axis=0), m, -1, same_ref, swap_ref)
        return carry

    lax.fori_loop(0, CHIPS // GROUP, holders, 0)
    end_sums(sum_ref, rows_ref)


def share_out(sum_refs, small_ref, keep_ref, send_ref):
    _, core = place_of()
    for r in range(NL):
        for k, ref in enumerate(sum_refs):
            small_ref[r, 2 * k : 2 * k + 2, :] = ref[CH + 2 * r : CH + 2 * r + 2, :]
        small_ref[r, 6:8, :] = jnp.zeros((2, CH), F32)
    for side, out in ((core, keep_ref), (1 - core, send_ref)):
        for piece in range(CHIPS):
            r = 2 * piece + side
            for k, ref in enumerate(sum_refs):
                out[piece, k * 16 : (k + 1) * 16, :] = ref[pl.ds(pl.multiple_of(r * 16, 16), 16), :]
            out[piece, 48:SHARE, :] = small_ref[r]


def backward_kernel(k, *refs):
    in_ref, in_swap_ref, x_ref = refs[:3]
    saved = refs[3:7]
    gain_ref, taps_ref, mix_ref, order_ref, starts_ref = refs[7:12]
    if k == 1:
        same_ref, swap_ref, sum_ref, pad, rows_ref, grad_ref, hidden_ref = refs[12:]
    else:
        sum1_ref, sum2_ref, first_ref, second_ref = refs[12:16]
        imitated_ref, own_ref, home_ref, keep_ref, send_ref = refs[16:21]
        pad, rows_ref, grad_ref, hidden_ref, sum_ref, small_ref = refs[21:]
        zone, core = place_of()
        for m in range(CHIPS):
            for ref, first in ((first_ref, 2 * m - core), (second_ref, 2 * m + 1 - 3 * core)):
                b = jnp.bitwise_and(first - 4 * zone + 4 * NL, NL - 1)
                imitated_ref[0, pl.ds(pl.multiple_of(b * Q, Q), Q), :] = ref[m]
    clear(pad)
    start_sums(sum_ref, rows_ref)

    def holders(i, carry):
        ms = [i * GROUP + g for g in range(GROUP)]
        rows = []
        for g, m in enumerate(ms):
            rows.append(block_row(order_ref[k, m], False))
            gather_stage(rows[-1], moved_rows(in_ref, in_swap_ref, m), grad_ref.at[g])
        for g, m in enumerate(ms):
            slope_stage(k, grad_ref.at[g], saved[3].at[m], hidden_ref.at[g], mix_ref)
        for g, m in enumerate(ms):
            sums = [None] * (TAPS + 1)
            grads = [
                backward_line(
                    k,
                    grad_ref.at[g],
                    x_ref.at[m],
                    starts_ref.at[k, m],
                    at(saved, m),
                    hidden_ref.at[g],
                    gain_ref,
                    taps_ref,
                    pad.at[g],
                    line,
                    sums,
                )
                for line in range(LINES)
            ]
            add_sums(sum_ref, rows_ref, saved[0].at[m], grad_ref.at[g], sums)
            values = jnp.concatenate(grads, axis=0)
            if k == 1:
                put_next(rows[g], values, m, -1, same_ref, swap_ref)
            else:
                put_home(rows[g], values, m, own_ref, home_ref)
        return carry

    lax.fori_loop(0, CHIPS // GROUP, holders, 0)
    end_sums(sum_ref, rows_ref)
    if k == 0:
        share_out((sum_ref, sum1_ref, sum2_ref), small_ref, keep_ref, send_ref)


def finish_kernel(own_ref, other_ref, grad_ref, home_ref, mix_ref, taps_ref, gain_ref, out_ref, tail_ref):
    _, core = place_of()
    for m in range(CHIPS):
        for ref, b in ((grad_ref, 2 * m + core), (home_ref, 2 * m + 1 - core)):
            out_ref[0, pl.ds(pl.multiple_of(b * Q, Q), Q), :] = ref[m]
    for ref, side in ((own_ref, core), (other_ref, 1 - core)):
        for piece in range(CHIPS):
            r = 2 * piece + side
            for k in range(3):
                mix_ref[k, pl.ds(pl.multiple_of(r * 16, 16), 16), :] = ref[piece, k * 16 : (k + 1) * 16, :]
            tail_ref[r] = ref[piece, 48:SHARE, :]
    for k in range(3):
        for r in range(NL):
            pair = tail_ref[r, 2 * k : 2 * k + 2, :]
            if r < NL - 1:
                taps_ref[k, 2 * r : 2 * r + 2, :] = pair
            else:
                taps_ref[k, 2 * r : 2 * r + 1, :] = pair[0:1]
                gain_ref[k : k + 1, :] = pair[1:2]


def call(kernel, outs, n_in, scratch=(), space=pltpu.VMEM, grant=VMEM_GRANT):
    vmem = pl.BlockSpec(memory_space=pltpu.VMEM)
    return pl.pallas_call(
        kernel,
        out_shape=outs,
        in_specs=[pl.BlockSpec(memory_space=space)] * n_in,
        out_specs=[vmem] * len(outs),
        scratch_shapes=[pltpu.VMEM(dims, F32) if isinstance(dims, tuple) else dims for dims in scratch],
        compiler_params=pltpu.CompilerParams(vmem_limit_bytes=grant),
    )


def shape(*dims, dtype=BF16):
    return jax.ShapeDtypeStruct(dims, dtype)


def swap(values):
    return lax.ppermute(values, "line", [(i, i ^ 1) for i in range(NL)])


def from_chips(values):
    got = [values]
    for back in range(1, CHIPS):
        got.append(lax.ppermute(values, "line", [(i, (i + 2 * back) % NL) for i in range(NL)]))
    return got


def to_ring(values, turn, ring, stride):
    pairs = []
    for i in range(lax.axis_size("dp")):
        at = i // stride % ring
        pairs.append((i, i + ((at + turn) % ring - at) * stride))
    return lax.ppermute(values, "dp", pairs)


def sum_over_dp(part):
    size = lax.axis_size("dp")
    stride = 1
    while stride < size:
        ring = RING if size % (stride * RING) == 0 else 2
        own = lax.reduce_precision(part, exponent_bits=8, mantissa_bits=7)
        sent = own.astype(BF16)
        got = [to_ring(sent, turn, ring, stride).astype(F32) for turn in range(1, ring)]
        part = own + got[0] if ring == 2 else (own + got[1]) + (got[0] + got[2])
        stride *= ring
    return part


def block(fields, cotangent, norm_gain, kernel, mix_weight, line_order, line_starts):
    dp_size = lax.axis_size("dp")
    weights = (norm_gain, kernel, mix_weight)
    quarter = shape(CHIPS, Q, CH)
    moving = shape(CHIPS, CHIPS, Q, CH)
    tables = (shape(3, CHIPS, 1, CELLS, dtype=I32), shape(3, CHIPS, LINES, CH, dtype=F32))
    kinds = (BF16, BF16, BF16, F32, F32)
    state = [shape(CHIPS, LINES, LINE, CH, dtype=kind) for kind in kinds]
    sums = shape(ROWS, CH, dtype=F32)
    pad = (GROUP, LINES, LINE + 16, CH)
    lines = pltpu.VMEM((GROUP, LINES, LINE, CH), BF16)
    parts = (TAPS + 1, 8, CH)
    back = (pad, parts, lines, lines)
    wide = (GROUP, LINES, LINE, CH)

    keep, keep_cot, send, extra = call(
        prep_kernel,
        (quarter, quarter, shape(NL, Q, CH), shape(EXTRA, CH)),
        4,
        scratch=(pltpu.VMEM((3, CELLS), I32), pltpu.VMEM((3, LINES), I32), pltpu.SemaphoreType.DMA((18,))),
        space=pltpu.HBM,
        grant=None,
    )(fields, cotangent, line_order, line_starts)
    got = swap(send)
    piece = jnp.concatenate([keep.reshape(HALF, CH), got[:CHIPS].reshape(HALF, CH), extra])
    piece_cot = jnp.concatenate([keep_cot.reshape(HALF, CH), got[CHIPS:].reshape(HALF, CH)])
    pieces = from_chips(piece)
    pieces_cot = from_chips(piece_cot)
    order, starts, same, moved, *saved0 = call(
        functools.partial(forward_kernel, 0), (*tables, moving, moving, *state), 7, scratch=(pad,)
    )(*pieces, *weights)
    given = (*weights, order, starts)
    same, moved, *saved1 = call(
        functools.partial(forward_kernel, 1), (moving, moving, *state), 7, scratch=(pad,)
    )(same, swap(moved), *given)
    same, moved, first, second, sums2 = call(
        turn_kernel, (moving, moving, quarter, quarter, sums), 11, scratch=(*back, lines, lines, lines, wide, wide)
    )(same, swap(moved), *pieces_cot, *given)
    second = swap(second)
    moved = swap(moved)
    same, moved, sums1 = call(
        functools.partial(backward_kernel, 1), (moving, moving, sums), 12, scratch=back
    )(same, moved, *saved1, *given)
    share = shape(CHIPS, SHARE, CH, dtype=F32)
    imitated, own, home, keep, send = call(
        functools.partial(backward_kernel, 0),
        (shape(1, CELLS, CH), quarter, quarter, share, share),
        16,
        scratch=(*back, (ROWS, CH), (NL, 8, CH)),
    )(same, swap(moved), *saved0, *given, sums1, sums2, first, second)
    grad_scale = float(dp_size * NL * CELLS) ** (-0.5)
    got = swap(send)
    home = swap(home)
    shares = sum_over_dp(keep + got) * grad_scale
    mix_grad, kernel_grad, gain_grad, field_grad = call(
        finish_kernel,
        (
            shape(3, CH, CH, dtype=F32),
            shape(3, TAPS, CH, dtype=F32),
            shape(3, CH, dtype=F32),
            shape(1, CELLS, CH),
        ),
        4,
        scratch=((NL, 8, CH),),
    )(shares, swap(shares), own, home)
    return imitated, field_grad, mix_grad, kernel_grad, gain_grad


def solution(mesh):
    in_specs = (
        P("dp", "line", None),
        P("dp", "line", None),
        P(),
        P(),
        P(),
        P(None, "line"),
        P(None, "line"),
    )
    out_specs = (P("dp", "line", None), P("dp", "line", None), P(), P(), P())
    return jax.shard_map(block, mesh=mesh, in_specs=in_specs, out_specs=out_specs, check_vma=False)
```

```python
import functools

import jax
import jax.numpy as jnp
from jax import lax
from jax.experimental import pallas as pl
from jax.experimental.pallas import tpu as pltpu
from jax.sharding import PartitionSpec as P


LINE = 128
CH = 128
TAPS = 15
CELLS = 512
NL = 8
CHIPS = NL // 2
RING = 4
GROUP = 2
Q = CELLS // NL
HALF = CELLS // 2
LINES = CELLS // LINE
EPSILON = 1e-06
OFFSETS = [0] + [s * 2**level for level in range(7) for s in (-1, 1)]
F32 = jnp.float32
BF16 = jnp.bfloat16
I32 = jnp.int32
ROWS = LINE + TAPS + 1
EXTRA = 48
SHARE = 56
VMEM_GRANT = 12 * 2**20


def dot(a, b, ca, cb):
    return lax.dot_general(a, b, (((ca,), (cb,)), ((), ())), preferred_element_type=F32)


def place_of():
    me = lax.axis_index("line")
    return lax.shift_right_logical(me, 1), jnp.bitwise_and(me, 1)


def wrap(index):
    return jnp.bitwise_and(index, CHIPS - 1)


def block_row(order, gathered):
    home = lax.shift_right_logical(order, 6)
    within = jnp.bitwise_and(order, Q - 1)
    odd = jnp.bitwise_and(home, 1)
    chip = lax.shift_right_logical(home, 1)
    if gathered:
        zone, core = place_of()
        odd = jnp.bitwise_xor(odd, core)
        chip = wrap(zone - chip + CHIPS)
    return odd * HALF + chip * Q + within


def picks(row, line):
    part = row[:, line * LINE : (line + 1) * LINE]
    wanted = jnp.transpose(jnp.broadcast_to(part, (LINE, LINE)))
    lanes = lax.broadcasted_iota(I32, (LINE, LINE), 1)
    return jnp.concatenate(
        [jnp.where(wanted == lanes + c * LINE, 1.0, 0.0).astype(BF16) for c in range(LINES)],
        axis=1,
    )


def place(row, values, rows):
    hot = jnp.where(jnp.broadcast_to(row, (LINE, CELLS)) == rows, 1.0, 0.0).astype(BF16)
    return dot(hot, values, 1, 0).astype(BF16)


def put_next(row, values, m, sign, same_ref, swap_ref):
    _, core = place_of()
    for c in range(LINES):
        rows = lax.broadcasted_iota(I32, (LINE, CELLS), 0) + c * LINE
        placed = place(row, values, rows)
        for half in range(2):
            h = (c * 2 + half) % CHIPS
            block = placed[half * Q : (half + 1) * Q]
            if c < LINES // 2:
                same_ref[wrap(m + sign * h + CHIPS), h] = block
            else:
                at = m + h + core if sign > 0 else m - h - 1 + core + CHIPS
                swap_ref[wrap(at), h] = block


def put_home(row, values, m, own_ref, swap_ref):
    zone, core = place_of()
    step = lax.broadcasted_iota(I32, (LINE, CELLS), 0)
    mine = (core * CHIPS + zone) * Q
    other = ((1 - core) * CHIPS + zone) * Q - Q
    placed = place(row, values, step + jnp.where(step < Q, mine, other))
    own_ref[m] = placed[:Q]
    swap_ref[m] = placed[Q:]


def shifts(pad, values):
    pad[8 : 8 + LINE, :] = values
    for offset in OFFSETS:
        if offset == 0:
            yield 0, values
        elif abs(offset) < 8:
            yield 0, pad[8 + offset : 8 + offset + LINE, :]
        elif offset > 0:
            yield 0, values[offset:]
        else:
            yield -offset, values[:offset]


def accumulate(total, first, rows):
    size = rows.shape[0]
    pieces = [total[:first]] if first else []
    pieces.append(total[first : first + size] + rows)
    if first + size < LINE:
        pieces.append(total[first + size :])
    return jnp.concatenate(pieces, axis=0) if len(pieces) > 1 else pieces[0]


def clear(pads):
    edge = jnp.zeros((GROUP, LINES, 8, CH), F32)
    pads[:, :, 0:8, :] = edge
    pads[:, :, 8 + LINE : 16 + LINE, :] = edge


def norm(x, gain, start):
    inverse = lax.rsqrt(jnp.mean(x * x, axis=-1, keepdims=True) + EPSILON)
    scaled = x * inverse
    normed = (scaled * gain).astype(BF16).astype(F32)
    return inverse, jnp.where(kept(start), normed, 0.0)


def kept(start):
    return lax.broadcasted_iota(I32, (LINE, CH), 0).astype(F32) >= start


def conv(pad, masked, taps):
    total = None
    for t, (first, moved) in enumerate(shifts(pad, masked)):
        term = taps[t : t + 1, :] * moved
        total = term if total is None else accumulate(total, first, term)
    return total


def sigmoid(h):
    return 1.0 / (1.0 + jnp.exp(-h))


def gather_stage(row, received, out):
    for line in range(LINES):
        out[line] = dot(picks(row, line), received, 1, 0).astype(BF16)


def hidden_stage(k, x_at, start_at, saved, gain_ref, taps_ref, pads, line):
    active, masked_at, inverse_at, slope_at = saved
    x = x_at[line].astype(F32)
    inverse, masked = norm(x, gain_ref[k : k + 1, :], start_at[line : line + 1, :])
    hidden = conv(pads.at[line], masked, taps_ref[k])
    gate = sigmoid(hidden)
    active[line] = (hidden * gate).astype(BF16)
    masked_at[line] = masked.astype(BF16)
    inverse_at[line] = jnp.broadcast_to(inverse, (LINE, CH))
    slope_at[line] = gate * (1.0 + hidden * (1.0 - gate))


def mix_stage(k, x_at, active, mix_ref):
    mixed = dot(active[...].reshape(CELLS, CH), mix_ref[k], 1, 0).astype(BF16).astype(F32)
    return (x_at[...].reshape(CELLS, CH).astype(F32) + mixed).astype(BF16)


def slope_stage(k, grad_at, slope_at, out, mix_ref):
    grad_act = dot(grad_at[...].reshape(CELLS, CH), mix_ref[k], 1, 1).reshape(LINES, LINE, CH)
    for line in range(LINES):
        out[line] = (grad_act[line] * slope_at[line]).astype(BF16)


def backward_line(k, grad_at, x_at, start_at, saved, hidden_at, gain_ref, taps_ref, pads, line, sums):
    gain = gain_ref[k : k + 1, :]
    taps = taps_ref[k]
    masked = saved[1][line].astype(F32)
    inverse = saved[2][line]
    scaled = x_at[line].astype(F32) * inverse
    keep = kept(start_at[line : line + 1, :])
    total = None
    for t, (first, moved) in enumerate(shifts(pads.at[line], hidden_at[line].astype(F32))):
        u = t if t == 0 else (t + 1 if t % 2 else t - 1)
        size = moved.shape[0]
        term = taps[u : u + 1, :] * moved
        total = term if total is None else accumulate(total, first, term)
        part = jnp.sum((moved * masked[first : first + size]).reshape(size // 8, 8, CH), axis=0)
        sums[u] = part if sums[u] is None else sums[u] + part
    cells = jnp.where(keep, total, 0.0).astype(BF16).astype(F32)
    part = jnp.sum((cells * scaled).reshape(LINE // 8, 8, CH), axis=0)
    sums[TAPS] = part if sums[TAPS] is None else sums[TAPS] + part
    weighted = cells * gain
    moved = inverse * (weighted - scaled * jnp.mean(weighted * scaled, axis=-1, keepdims=True))
    return (grad_at[line].astype(F32) + moved).astype(BF16)


def at(saved, index):
    return [ref.at[index] for ref in saved]


def add_sums(sum_ref, rows_ref, active, grad_at, sums):
    sum_ref[0:CH, :] += dot(active[...].reshape(CELLS, CH), grad_at[...].reshape(CELLS, CH), 0, 0)
    for t, part in enumerate(sums):
        rows_ref[t] += part


def start_sums(sum_ref, rows_ref):
    sum_ref[...] = jnp.zeros_like(sum_ref)
    rows_ref[...] = jnp.zeros_like(rows_ref)


def end_sums(sum_ref, rows_ref):
    sum_ref[CH:ROWS, :] = jnp.sum(rows_ref[...], axis=1)


def prep_kernel(fields_ref, cot_ref, table_ref, begin_ref, keep_ref, keep_cot_ref, send_ref, order_ref, starts_ref, sem):
    _, core = place_of()
    copies = [
        pltpu.make_async_copy(table_ref, order_ref, sem.at[0]),
        pltpu.make_async_copy(begin_ref, starts_ref, sem.at[1]),
    ]
    for m in range(CHIPS):
        here = pl.ds(pl.multiple_of((2 * m + core) * Q, Q), Q)
        there = pl.ds(pl.multiple_of((2 * m + 1 - core) * Q, Q), Q)
        for source, own, first in ((fields_ref, keep_ref, 0), (cot_ref, keep_cot_ref, CHIPS)):
            for rows, target in ((here, own.at[pl.ds(m * Q, Q), :]), (there, send_ref.at[first + m])):
                copies.append(pltpu.make_async_copy(source.at[0, rows, :], target, sem.at[len(copies)]))
    for copy in copies:
        copy.start()
    for copy in copies[:2]:
        copy.wait()
    rows = []
    for k in range(3):
        order = order_ref[k : k + 1, :]
        for part in (lax.shift_right_logical(order, 1), jnp.bitwise_and(order, 1)):
            rows += [part[:, c * LINE : (c + 1) * LINE].astype(F32) for c in range(LINES)]
    starts = starts_ref[...].astype(F32)
    for k in range(3):
        rows += [jnp.broadcast_to(starts[k : k + 1, line : line + 1], (1, CH)) for line in range(LINES)]
    rows.append(jnp.zeros((EXTRA - len(rows), CH), F32))
    keep_ref[HALF : HALF + EXTRA, :] = jnp.concatenate(rows, axis=0).astype(BF16)
    for copy in copies[2:]:
        copy.wait()


def read_tables(pieces, order_ref, starts_ref):
    zone, _ = place_of()
    for back, ref in enumerate(pieces):
        m = wrap(zone - back + CHIPS)
        extra = ref[CELLS : CELLS + EXTRA, :].astype(F32)
        for k in range(3):
            for c in range(LINES):
                high = extra[8 * k + c : 8 * k + c + 1]
                low = extra[8 * k + 4 + c : 8 * k + 5 + c]
                order_ref[k, m, :, c * LINE : (c + 1) * LINE] = (2.0 * high + low).astype(I32)
            starts_ref[k, m] = extra[24 + 4 * k : 28 + 4 * k]


def gathered_rows(pieces, m, k):
    zone, core = place_of()
    rows = []
    for odd in range(2):
        for back, ref in enumerate(pieces):
            home = 2 * (zone - back) + jnp.bitwise_xor(core, odd)
            block = wrap(m - (k // 2) * home + NL)
            rows.append(ref[pl.ds(pl.multiple_of(odd * HALF + block * Q, Q), Q), :])
    return jnp.concatenate(rows, axis=0)


def moved_rows(same_ref, swap_ref, m):
    return jnp.concatenate([same_ref[m].reshape(HALF, CH), swap_ref[m].reshape(HALF, CH)], axis=0)


def forward_kernel(k, *refs):
    if k == 0:
        pieces, refs = refs[:CHIPS], refs[CHIPS:]
        gain_ref, taps_ref, mix_ref, order_ref, starts_ref, same_ref, swap_ref, x_ref, *saved, pad = refs
        read_tables(pieces, order_ref, starts_ref)
    else:
        in_ref, in_swap_ref, gain_ref, taps_ref, mix_ref, order_ref, starts_ref = refs[:7]
        same_ref, swap_ref, x_ref, *saved, pad = refs[7:]
    clear(pad)

    def holders(i, carry):
        ms = [i * GROUP + g for g in range(GROUP)]
        rows = []
        for m in ms:
            received = gathered_rows(pieces, m, k) if k == 0 else moved_rows(in_ref, in_swap_ref, m)
            rows.append(order_ref[k, m])
            gather_stage(block_row(rows[-1], k == 0), received, x_ref.at[m])
        for g, m in enumerate(ms):
            for line in range(LINES):
                hidden_stage(
                    k, x_ref.at[m], starts_ref.at[k, m], at(saved, m), gain_ref, taps_ref, pad.at[g], line
                )
        after = [mix_stage(k, x_ref.at[m], saved[0].at[m], mix_ref) for m in ms]
        for g, m in enumerate(ms):
            put_next(block_row(rows[g], False), after[g], m, 1, same_ref, swap_ref)
        return carry

    lax.fori_loop(0, CHIPS // GROUP, holders, 0)


def turn_kernel(*refs):
    k = 2
    in_ref, in_swap_ref = refs[:2]
    pieces = refs[2 : 2 + CHIPS]
    gain_ref, taps_ref, mix_ref, order_ref, starts_ref = refs[2 + CHIPS : 7 + CHIPS]
    same_ref, swap_ref, own_ref, home_ref, sum_ref = refs[7 + CHIPS : 12 + CHIPS]
    pad, rows_ref, grad_ref, hidden_ref, x_ref, *saved = refs[12 + CHIPS :]
    clear(pad)
    start_sums(sum_ref, rows_ref)

    def holders(i, carry):
        ms = [i * GROUP + g for g in range(GROUP)]
        rows = []
        for g, m in enumerate(ms):
            order = order_ref[k, m]
            rows.append(block_row(order, False))
            gather_stage(rows[-1], moved_rows(in_ref, in_swap_ref, m), x_ref.at[g])
            gather_stage(block_row(order, True), gathered_rows(pieces, m, k), grad_ref.at[g])
        for g, m in enumerate(ms):
            for line in range(LINES):
                hidden_stage(
                    k, x_ref.at[g], starts_ref.at[k, m], at(saved, g), gain_ref, taps_ref, pad.at[g], line
                )
        for g, m in enumerate(ms):
            after = mix_stage(k, x_ref.at[g], saved[0].at[g], mix_ref)
            slope_stage(k, grad_ref.at[g], saved[3].at[g], hidden_ref.at[g], mix_ref)
            put_home(rows[g], after, m, own_ref, home_ref)
        for g, m in enumerate(ms):
            sums = [None] * (TAPS + 1)
            grads = [
                backward_line(
                    k,
                    grad_ref.at[g],
                    x_ref.at[g],
                    starts_ref.at[k, m],
                    at(saved, g),
                    hidden_ref.at[g],
                    gain_ref,
                    taps_ref,
                    pad.at[g],
                    line,
                    sums,
                )
                for line in range(LINES)
            ]
            add_sums(sum_ref, rows_ref, saved[0].at[g], grad_ref.at[g], sums)
            put_next(rows[g], jnp.concatenate(grads, axis=0), m, -1, same_ref, swap_ref)
        return carry

    lax.fori_loop(0, CHIPS // GROUP, holders, 0)
    end_sums(sum_ref, rows_ref)


def share_out(sum_refs, small_ref, keep_ref, send_ref):
    _, core = place_of()
    for r in range(NL):
        for k, ref in enumerate(sum_refs):
            small_ref[r, 2 * k : 2 * k + 2, :] = ref[CH + 2 * r : CH + 2 * r + 2, :]
        small_ref[r, 6:8, :] = jnp.zeros((2, CH), F32)
    for side, out in ((core, keep_ref), (1 - core, send_ref)):
        for piece in range(CHIPS):
            r = 2 * piece + side
            for k, ref in enumerate(sum_refs):
                out[piece, k * 16 : (k + 1) * 16, :] = ref[pl.ds(pl.multiple_of(r * 16, 16), 16), :]
            out[piece, 48:SHARE, :] = small_ref[r]


def backward_kernel(k, *refs):
    in_ref, in_swap_ref, x_ref = refs[:3]
    saved = refs[3:7]
    gain_ref, taps_ref, mix_ref, order_ref, starts_ref = refs[7:12]
    if k == 1:
        same_ref, swap_ref, sum_ref, pad, rows_ref, grad_ref, hidden_ref = refs[12:]
    else:
        sum1_ref, sum2_ref, first_ref, second_ref = refs[12:16]
        imitated_ref, own_ref, home_ref, keep_ref, send_ref = refs[16:21]
        pad, rows_ref, grad_ref, hidden_ref, sum_ref, small_ref = refs[21:]
        zone, core = place_of()
        for m in range(CHIPS):
            for ref, first in ((first_ref, 2 * m - core), (second_ref, 2 * m + 1 - 3 * core)):
                b = jnp.bitwise_and(first - 4 * zone + 4 * NL, NL - 1)
                imitated_ref[0, pl.ds(pl.multiple_of(b * Q, Q), Q), :] = ref[m]
    clear(pad)
    start_sums(sum_ref, rows_ref)

    def holders(i, carry):
        ms = [i * GROUP + g for g in range(GROUP)]
        rows = []
        for g, m in enumerate(ms):
            rows.append(block_row(order_ref[k, m], False))
            gather_stage(rows[-1], moved_rows(in_ref, in_swap_ref, m), grad_ref.at[g])
        for g, m in enumerate(ms):
            slope_stage(k, grad_ref.at[g], saved[3].at[m], hidden_ref.at[g], mix_ref)
        for g, m in enumerate(ms):
            sums = [None] * (TAPS + 1)
            grads = [
                backward_line(
                    k,
                    grad_ref.at[g],
                    x_ref.at[m],
                    starts_ref.at[k, m],
                    at(saved, m),
                    hidden_ref.at[g],
                    gain_ref,
                    taps_ref,
                    pad.at[g],
                    line,
                    sums,
                )
                for line in range(LINES)
            ]
            add_sums(sum_ref, rows_ref, saved[0].at[m], grad_ref.at[g], sums)
            values = jnp.concatenate(grads, axis=0)
            if k == 1:
                put_next(rows[g], values, m, -1, same_ref, swap_ref)
            else:
                put_home(rows[g], values, m, own_ref, home_ref)
        return carry

    lax.fori_loop(0, CHIPS // GROUP, holders, 0)
    end_sums(sum_ref, rows_ref)
    if k == 0:
        share_out((sum_ref, sum1_ref, sum2_ref), small_ref, keep_ref, send_ref)


def finish_kernel(own_ref, other_ref, grad_ref, home_ref, mix_ref, taps_ref, gain_ref, out_ref, tail_ref):
    _, core = place_of()
    for m in range(CHIPS):
        for ref, b in ((grad_ref, 2 * m + core), (home_ref, 2 * m + 1 - core)):
            out_ref[0, pl.ds(pl.multiple_of(b * Q, Q), Q), :] = ref[m]
    for ref, side in ((own_ref, core), (other_ref, 1 - core)):
        for piece in range(CHIPS):
            r = 2 * piece + side
            for k in range(3):
                mix_ref[k, pl.ds(pl.multiple_of(r * 16, 16), 16), :] = ref[piece, k * 16 : (k + 1) * 16, :]
            tail_ref[r] = ref[piece, 48:SHARE, :]
    for k in range(3):
        for r in range(NL):
            pair = tail_ref[r, 2 * k : 2 * k + 2, :]
            if r < NL - 1:
                taps_ref[k, 2 * r : 2 * r + 2, :] = pair
            else:
                taps_ref[k, 2 * r : 2 * r + 1, :] = pair[0:1]
                gain_ref[k : k + 1, :] = pair[1:2]


def call(kernel, outs, n_in, scratch=(), space=pltpu.VMEM, grant=VMEM_GRANT):
    vmem = pl.BlockSpec(memory_space=pltpu.VMEM)
    return pl.pallas_call(
        kernel,
        out_shape=outs,
        in_specs=[pl.BlockSpec(memory_space=space)] * n_in,
        out_specs=[vmem] * len(outs),
        scratch_shapes=[pltpu.VMEM(dims, F32) if isinstance(dims, tuple) else dims for dims in scratch],
        compiler_params=pltpu.CompilerParams(vmem_limit_bytes=grant),
    )


def shape(*dims, dtype=BF16):
    return jax.ShapeDtypeStruct(dims, dtype)


def swap(values):
    return lax.ppermute(values, "line", [(i, i ^ 1) for i in range(NL)])


def from_chips(values):
    got = [values]
    for back in range(1, CHIPS):
        got.append(lax.ppermute(values, "line", [(i, (i + 2 * back) % NL) for i in range(NL)]))
    return got


def to_ring(values, turn, ring, stride):
    pairs = []
    for i in range(lax.axis_size("dp")):
        at = i // stride % ring
        pairs.append((i, i + ((at + turn) % ring - at) * stride))
    return lax.ppermute(values, "dp", pairs)


def sum_over_dp(part):
    size = lax.axis_size("dp")
    stride = 1
    while stride < size:
        ring = RING if size % (stride * RING) == 0 else 2
        own = lax.reduce_precision(part, exponent_bits=8, mantissa_bits=7)
        sent = own.astype(BF16)
        got = [to_ring(sent, turn, ring, stride).astype(F32) for turn in range(1, ring)]
        part = own + got[0] if ring == 2 else (own + got[1]) + (got[0] + got[2])
        stride *= ring
    return part


def block(fields, cotangent, norm_gain, kernel, mix_weight, line_order, line_starts):
    dp_size = lax.axis_size("dp")
    weights = (norm_gain, kernel, mix_weight)
    quarter = shape(CHIPS, Q, CH)
    moving = shape(CHIPS, CHIPS, Q, CH)
    tables = (shape(3, CHIPS, 1, CELLS, dtype=I32), shape(3, CHIPS, LINES, CH, dtype=F32))
    kinds = (BF16, BF16, BF16, F32, F32)
    state = [shape(CHIPS, LINES, LINE, CH, dtype=kind) for kind in kinds]
    sums = shape(ROWS, CH, dtype=F32)
    pad = (GROUP, LINES, LINE + 16, CH)
    lines = pltpu.VMEM((GROUP, LINES, LINE, CH), BF16)
    parts = (TAPS + 1, 8, CH)
    back = (pad, parts, lines, lines)
    wide = (GROUP, LINES, LINE, CH)

    keep, keep_cot, send = call(
        prep_kernel,
        (shape(HALF + EXTRA, CH), shape(HALF, CH), shape(NL, Q, CH)),
        4,
        scratch=(pltpu.VMEM((3, CELLS), I32), pltpu.VMEM((3, LINES), I32), pltpu.SemaphoreType.DMA((18,))),
        space=pltpu.HBM,
        grant=None,
    )(fields, cotangent, line_order, line_starts)
    got = swap(send)
    piece = jnp.concatenate([keep[:HALF], got[:CHIPS].reshape(HALF, CH), keep[HALF:]])
    piece_cot = jnp.concatenate([keep_cot, got[CHIPS:].reshape(HALF, CH)])
    pieces = from_chips(piece)
    pieces_cot = from_chips(piece_cot)
    order, starts, same, moved, *saved0 = call(
        functools.partial(forward_kernel, 0), (*tables, moving, moving, *state), 7, scratch=(pad,)
    )(*pieces, *weights)
    given = (*weights, order, starts)
    same, moved, *saved1 = call(
        functools.partial(forward_kernel, 1), (moving, moving, *state), 7, scratch=(pad,)
    )(same, swap(moved), *given)
    same, moved, first, second, sums2 = call(
        turn_kernel, (moving, moving, quarter, quarter, sums), 11, scratch=(*back, lines, lines, lines, wide, wide)
    )(same, swap(moved), *pieces_cot, *given)
    second = swap(second)
    moved = swap(moved)
    same, moved, sums1 = call(
        functools.partial(backward_kernel, 1), (moving, moving, sums), 12, scratch=back
    )(same, moved, *saved1, *given)
    share = shape(CHIPS, SHARE, CH, dtype=F32)
    imitated, own, home, keep, send = call(
        functools.partial(backward_kernel, 0),
        (shape(1, CELLS, CH), quarter, quarter, share, share),
        16,
        scratch=(*back, (ROWS, CH), (NL, 8, CH)),
    )(same, swap(moved), *saved0, *given, sums1, sums2, first, second)
    grad_scale = float(dp_size * NL * CELLS) ** (-0.5)
    got = swap(send)
    home = swap(home)
    shares = sum_over_dp(keep + got) * grad_scale
    mix_grad, kernel_grad, gain_grad, field_grad = call(
        finish_kernel,
        (
            shape(3, CH, CH, dtype=F32),
            shape(3, TAPS, CH, dtype=F32),
            shape(3, CH, dtype=F32),
            shape(1, CELLS, CH),
        ),
        4,
        scratch=((NL, 8, CH),),
    )(shares, swap(shares), own, home)
    return imitated, field_grad, mix_grad, kernel_grad, gain_grad


def solution(mesh):
    in_specs = (
        P("dp", "line", None),
        P("dp", "line", None),
        P(),
        P(),
        P(),
        P(None, "line"),
        P(None, "line"),
    )
    out_specs = (P("dp", "line", None), P("dp", "line", None), P(), P(), P())
    return jax.shard_map(block, mesh=mesh, in_specs=in_specs, out_specs=out_specs, check_vma=False)
```
